256 devices in a mesh: dp: 32 (over x, z), tensor: 8 (over y, core).
Axes of the slice: x: 4, y: 4, z: 8, core: 2. Of those that a mesh axis runs over, the one named last changes fastest.
Arguments:
- context: bfloat16 [2, 32768, 3072], P(None, 'dp', 'tensor'), may hold values from -6 to 6
- out_grad: bfloat16 [2, 32768, 3072], P(None, ('dp', 'tensor')), may hold values from -0.1875 to 0.1875
- error_in: bfloat16 [2, 98304, 3072], P(None, 'dp', 'tensor'), may hold values from -6 to 6
- right_init: float32 [2, 64, 3072], P(None, None, 'tensor'), may hold values from -6 to 6
Outputs:
- summed_update: bfloat16 [2, 3072, 3072], P(None, 'dp', 'tensor')
- error_out: bfloat16 [2, 98304, 3072], P(None, 'dp', 'tensor')
The draws below stay inside these ranges and needn't reach their ends.
All inputs are finite; a program needn't handle non-finite values.
Results may differ from the reference program's by a relative error of at most 0.015.
Values may be sent and summed in bfloat16 or wider, within the bound.
No kernel may reach another device: no remote copies, remote signals or barrier semaphores. Data moves between devices by JAX's collectives and lax.ppermute only.
A program may use at most 128 MiB of HBM per device.

```python
import jax
import jax.numpy as jnp
from jax import lax

D = 3072
RANK = 64
LAYERS = 2
TOK_DEV = 1024
TOKENS = 32768
REPL_ROWS = 98304
N_DP = 32


def block_levels(key, shape, pieces, least, high):
    loudness = 1.0
    for dim, blocks in pieces:
        heights = jax.random.uniform(jax.random.fold_in(jax.random.fold_in(key, 6), dim), (blocks,), jnp.float32, least / len(pieces), high / len(pieces))
        loudness = loudness * jnp.repeat(jnp.exp(heights), shape[dim] // blocks).reshape((-1,) + (1,) * (len(shape) - 1 - dim))
    return loudness


def scatter_about(rng, dims, deviation, bound, split=(), held_as=jnp.bfloat16):
    result = jax.random.normal(rng, dims, jnp.float32) * deviation
    if len(split) > 0:
        result = block_levels(rng, dims, split, -0.22, 0.18) * result
    return jnp.clip(result, min=-bound, max=bound).astype(held_as)


def setup_inputs(seed: int = 0) -> dict:
    keys = jax.random.split(jax.random.key(seed), 5)
    context = scatter_about(keys[0], (LAYERS, TOKENS, D), 1.0, 6.0, ((1, 32), (2, 8)))
    out_grad = scatter_about(keys[1], (LAYERS, TOKENS, D), TOK_DEV ** -0.5, 0.1875, ((1, 256),))
    error_in = scatter_about(keys[2], (LAYERS, REPL_ROWS, D), 1.0, 6.0, ((1, 32), (2, 8)))
    right_init = scatter_about(keys[3], (LAYERS, RANK, D), 1.0, 6.0, ((2, 8),), jnp.float32)
    return {"context": context, "out_grad": out_grad, "error_in": error_in, "right_init": right_init}


def ortho_rows(left_factor):
    gram_matrix = jnp.dot(left_factor, left_factor.T, precision=lax.Precision.HIGHEST)
    ridge_term = 1e-06 * jnp.mean(jnp.diagonal(gram_matrix))
    gram_matrix = gram_matrix + ridge_term * jnp.eye(gram_matrix.shape[0], dtype=gram_matrix.dtype)
    factor_low = jnp.linalg.cholesky(gram_matrix)
    return jax.scipy.linalg.solve_triangular(factor_low, left_factor, lower=True)

def reference(context, out_grad, error_in, right_init):
    summed_list = []
    error_list = []
    for layer in range(LAYERS):
        ctx_blocks = context[layer].reshape(N_DP, TOK_DEV, D)
        grad_blocks = out_grad[layer].reshape(N_DP, TOK_DEV, D)
        err_blocks = error_in[layer].reshape(N_DP, D, D)

        def one_moment(items):
            return jnp.dot(items[1].T.astype(jnp.float32), items[0].astype(jnp.float32), preferred_element_type=jnp.float32) + items[2].astype(jnp.float32)
        moments = lax.map(one_moment, (ctx_blocks, grad_blocks, err_blocks))
        left_factor = jnp.einsum('re,nde->rd', right_init[layer], moments, precision=lax.Precision.HIGHEST)
        ortho_basis = ortho_rows(left_factor)
        right_factor = jnp.einsum('rd,nde->re', ortho_basis, moments, precision=lax.Precision.HIGHEST)
        summed = jnp.dot(ortho_basis.T, right_factor, precision=lax.Precision.HIGHEST)
        summed_list.append(summed.astype(jnp.bfloat16))
        mean_part = jnp.dot(ortho_basis.T, right_factor / N_DP, precision=lax.Precision.HIGHEST)
        new_error = (moments - mean_part[None]).astype(jnp.bfloat16)
        error_list.append(new_error.reshape(N_DP * D, D))
    return (jnp.stack(summed_list), jnp.stack(error_list))
```

```python
import functools

import jax
import jax.numpy as jnp
from jax import lax
from jax.experimental import pallas as pl
from jax.experimental.pallas import tpu as pltpu
from jax.sharding import Mesh
from jax.sharding import PartitionSpec as P

TENSOR = ("tensor_0", "tensor_1")
DP_TENSOR = ("dp_0", "dp_1", "tensor_0", "tensor_1")
DP = ("dp_0", "dp_1")
WIDE = ("dp_0", "dp_1", "tensor_0")
F32, BF16 = jnp.float32, jnp.bfloat16
HIGHEST = lax.Precision.HIGHEST
VMEM = pl.BlockSpec(memory_space=pltpu.VMEM)
SMEM = pl.BlockSpec(memory_space=pltpu.SMEM)


def room(mib):
    return pltpu.CompilerParams(vmem_limit_bytes=mib * 1024 * 1024)


def cost(flops, nbytes):
    return pl.CostEstimate(flops=int(flops), bytes_accessed=int(nbytes), transcendentals=0)


def two_parts(x):
    high = x.astype(BF16)
    return high, (x - high.astype(F32)).astype(BF16)


def dot(a, b, dims, **kw):
    return lax.dot_general(a, b, (dims, ((), ())), preferred_element_type=F32, **kw)


def sketch_kernel(r_ref, x_ref, o_ref):
    rank = r_ref.shape[1]
    for layer in range(r_ref.shape[0]):
        stacked = jnp.concatenate(two_parts(r_ref[layer]), axis=0)
        z = dot(stacked, x_ref[layer], ((1,), (1,)))
        z = (z[:rank] + z[rank:]).astype(BF16)
        for j in range(o_ref.shape[0]):
            o_ref[j, layer] = z[:, j * 128 : (j + 1) * 128]


def sketch(right_init, context):
    layers, rank, _ = right_init.shape
    tokens = context.shape[1]
    return pl.pallas_call(
        sketch_kernel,
        out_shape=jax.ShapeDtypeStruct((tokens // 128, layers, rank, 128), BF16),
        in_specs=[VMEM, VMEM],
        out_specs=VMEM,
        cost_estimate=cost(4e8, 2e6),
        name="sketch",
        compiler_params=room(6),
    )(right_init, context)


def error_sketch_kernel(r_ref, e_ref, o_ref):
    rank = r_ref.shape[1]
    stacked = jnp.concatenate(two_parts(r_ref[0]), axis=0)
    z = dot(stacked, e_ref[0], ((1,), (1,)))
    o_ref[0] = z[:rank] + z[rank:]


def error_sketch(right_init, error_in):
    layers, rank, width = right_init.shape
    rows = error_in.shape[1]
    step = 768
    return pl.pallas_call(
        error_sketch_kernel,
        out_shape=jax.ShapeDtypeStruct((layers, rank, rows), F32),
        grid=(layers, rows // step),
        in_specs=[
            pl.BlockSpec((1, rank, width), lambda l, d: (l, 0, 0)),
            pl.BlockSpec((1, step, width), lambda l, d: (l, d, 0)),
        ],
        out_specs=pl.BlockSpec((1, rank, step), lambda l, d: (l, 0, d)),
        cost_estimate=cost(6e8, 7e6),
        name="error_sketch",
        compiler_params=room(6),
    )(right_init, error_in)


def left_term_kernel(core_ref, z_ref, y_ref, e_ref, send_ref, keep_ref):
    rank = z_ref.shape[2]
    core = core_ref[0]
    for which, out in ((1 - core, send_ref), (core, keep_ref)):
        z = z_ref[0, which].astype(F32)
        for j in range(1, z_ref.shape[0]):
            z = z + z_ref[j, which].astype(F32)
        t = dot(jnp.concatenate(two_parts(z), axis=0), y_ref[which], ((1,), (0,)))
        out[...] = (t[:rank] + t[rank:] + e_ref[which]).astype(BF16)


def left_term(core, z, own_grad, error_part):
    rank, rows = error_part.shape[1:]
    shape = jax.ShapeDtypeStruct((rank, rows), BF16)
    return pl.pallas_call(
        left_term_kernel,
        out_shape=(shape, shape),
        in_specs=[SMEM, VMEM, VMEM, VMEM],
        out_specs=(VMEM, VMEM),
        cost_estimate=cost(2e8, 5e6),
        name="left_term",
        compiler_params=room(12),
    )(core, z, own_grad, error_part)


def cut_kernel(a_ref, b_ref, o_ref):
    bands, lanes = a_ref.shape[0] // 16, a_ref.shape[1] // 128
    for i in range(bands):
        for j in range(lanes):
            rows, cols = slice(i * 16, i * 16 + 16), slice(j * 128, j * 128 + 128)
            both = a_ref[rows, cols].astype(F32) + b_ref[rows, cols].astype(F32)
            o_ref[i * lanes + j] = both.astype(BF16)
    for p in range(bands * lanes, o_ref.shape[0]):
        o_ref[p] = jnp.zeros(o_ref.shape[1:], BF16)


def cut(a, b, pieces):
    return pl.pallas_call(
        cut_kernel,
        out_shape=jax.ShapeDtypeStruct((pieces, 16, 128), BF16),
        in_specs=[VMEM, VMEM],
        out_specs=VMEM,
        cost_estimate=cost(4e5, 1.2e6),
        name="cut",
        compiler_params=room(4),
    )(a, b)


def sum_copies_kernel(x_ref, o_ref):
    parts = [x_ref[p].astype(F32) for p in range(4)]
    for p in range(4, x_ref.shape[0], 4):
        for q in range(4):
            parts[q] = parts[q] + x_ref[p + q].astype(F32)
    total = ((parts[0] + parts[1]) + (parts[2] + parts[3])).astype(BF16)
    for p in range(o_ref.shape[0]):
        o_ref[p] = total


def sum_copies(x):
    return pl.pallas_call(
        sum_copies_kernel,
        out_shape=jax.ShapeDtypeStruct(x.shape, BF16),
        in_specs=[VMEM],
        out_specs=VMEM,
        cost_estimate=cost(x.size, x.size * 4),
        name="sum_copies",
        compiler_params=room(4),
    )(x)


def moment_kernel(y_ref, x_ref, e_ref, o_ref):
    y = jnp.concatenate([y_ref[k, 0] for k in range(y_ref.shape[0])], axis=1)
    o_ref[0] = dot(y, x_ref[0], ((1,), (0,))) + e_ref[0].astype(F32)


def moment_of(grad_t, context, error_in):
    blocks, layers, rows, _ = grad_t.shape
    tokens, width = context.shape[1:]
    step = 512
    return pl.pallas_call(
        moment_kernel,
        out_shape=jax.ShapeDtypeStruct((layers, rows, width), F32),
        grid=(layers, rows // step),
        in_specs=[
            pl.BlockSpec((blocks, 1, step, 128), lambda l, d: (0, l, d, 0)),
            pl.BlockSpec((1, tokens, width), lambda l, d: (l, 0, 0)),
            pl.BlockSpec((1, step, width), lambda l, d: (l, d, 0)),
        ],
        out_specs=pl.BlockSpec((1, step, width), lambda l, d: (l, d, 0)),
        cost_estimate=cost(5e9, 28e6),
        name="moment",
        compiler_params=room(60),
    )(grad_t, context, error_in)


def join_kernel(core_ref, own_ref, other_ref, l_ref):
    core = core_ref[0]
    bands, lanes = l_ref.shape[1] // 16, l_ref.shape[2] // 128
    for which, ref in ((core, own_ref), (1 - core, other_ref)):
        for i in range(bands):
            for j in range(lanes):
                l_ref[which, i * 16 : i * 16 + 16, j * 128 : j * 128 + 128] = ref[i * lanes + j]


def join(core, own, other, rank, rows):
    return pl.pallas_call(
        join_kernel,
        out_shape=jax.ShapeDtypeStruct((2, rank, rows), BF16),
        in_specs=[SMEM, VMEM, VMEM],
        out_specs=VMEM,
        cost_estimate=cost(1e5, 2e6),
        name="join",
        compiler_params=room(4),
    )(core, own, other)


def right_term_kernel(l_ref, m_ref, o_ref, acc_ref):
    layer, d = pl.program_id(0), pl.program_id(1)
    part = dot(l_ref[0], m_ref[0].astype(BF16), ((1,), (0,)))

    @pl.when(d == 0)
    def _():
        acc_ref[...] = part

    @pl.when(d > 0)
    def _():
        acc_ref[...] += part

    @pl.when(d == pl.num_programs(1) - 1)
    def _():
        bands, lanes = acc_ref.shape[0] // 16, acc_ref.shape[1] // 128
        for i in range(bands):
            for j in range(lanes):
                piece = acc_ref[i * 16 : i * 16 + 16, j * 128 : j * 128 + 128]
                o_ref[(layer * bands + i) * lanes + j] = piece.astype(BF16)

    @pl.when((layer == 0) & (d == 0))
    def _():
        bands, lanes = acc_ref.shape[0] // 16, acc_ref.shape[1] // 128
        for p in range(2 * bands * lanes, o_ref.shape[0]):
            o_ref[p] = jnp.zeros(o_ref.shape[1:], BF16)


def right_term(left, moment, pieces):
    layers, rank, rows = left.shape
    width = moment.shape[2]
    step = 768
    return pl.pallas_call(
        right_term_kernel,
        out_shape=jax.ShapeDtypeStruct((pieces, 16, 128), BF16),
        grid=(layers, rows // step),
        in_specs=[
            pl.BlockSpec((1, rank, step), lambda l, d: (l, 0, d)),
            pl.BlockSpec((1, step, width), lambda l, d: (l, d, 0)),
        ],
        out_specs=pl.BlockSpec((pieces, 16, 128), lambda l, d: (0, 0, 0)),
        scratch_shapes=[pltpu.VMEM((rank, width), F32)],
        cost_estimate=cost(4e8, 10e6),
        name="right_term",
        compiler_params=room(50),
    )(left, moment)


def inverse_kernel(l_ref, o_ref):
    rank = l_ref.shape[1]
    row = lax.broadcasted_iota(jnp.int32, (rank, 2 * rank), 0)
    col = lax.broadcasted_iota(jnp.int32, (rank, 2 * rank), 1)
    work = []
    for layer in range(l_ref.shape[0]):
        left = l_ref[layer]
        gram = dot(left, left, ((1,), (1,)))
        wide = jnp.concatenate([gram, jnp.zeros((rank, rank), F32)], axis=1)
        diag = jnp.sum(jnp.where(row == col, wide, 0.0), axis=1, keepdims=True)
        ridge = 1e-6 * (jnp.sum(diag, axis=0, keepdims=True) / rank)
        wide = wide + jnp.where(row == col, ridge, 0.0)
        work.append(jnp.where(col == row + rank, 1.0, wide))
    for k in range(rank):
        for layer in range(len(work)):
            a = work[layer]
            pivot_row = a[k : k + 1, :] / a[k : k + 1, k : k + 1]
            column = a[:, k : k + 1]
            work[layer] = jnp.where(row == k, pivot_row, a - column * pivot_row)
    for layer in range(len(work)):
        o_ref[layer] = work[layer][:, rank:]


def inverse_of_gram(left):
    layers, rank, _ = left.shape
    return pl.pallas_call(
        inverse_kernel,
        out_shape=jax.ShapeDtypeStruct((layers, rank, rank), F32),
        in_specs=[VMEM],
        out_specs=VMEM,
        cost_estimate=cost(5e9, 2e6),
        name="gram_inverse",
        compiler_params=room(4),
    )(left)


def outputs_kernel(r_ref, g_ref, l_ref, own_ref, m_ref, s_ref, e_ref, q_ref, *, replicas):
    layer, d = pl.program_id(0), pl.program_id(1)
    rank, width = g_ref.shape[1], m_ref.shape[2]
    bands, lanes = rank // 16, width // 128

    @pl.when(d == 0)
    def _():
        rows = [
            jnp.concatenate([r_ref[(layer * bands + i) * lanes + j] for j in range(lanes)], axis=1)
            for i in range(bands)
        ]
        right = jnp.concatenate(rows, axis=0).astype(F32)
        q = dot(g_ref[0], right, ((1,), (0,)), precision=HIGHEST)
        q_ref[...] = jnp.concatenate(two_parts(q), axis=0)
        own = own_ref[0]
        s = dot(jnp.concatenate([own, own], axis=0), q_ref[...], ((0,), (0,)))
        s_ref[0] = s.astype(BF16)

    left = l_ref[0]
    both = jnp.concatenate([left, left], axis=0)
    mean = dot(both, q_ref[...], ((0,), (0,))) * (1.0 / replicas)
    e_ref[0] = (m_ref[0] - mean).astype(BF16)


def outputs(right, inverse, left, own_left, moment, replicas):
    layers, rows, width = moment.shape
    rank = left.shape[1]
    share = own_left.shape[2]
    step = 768
    return pl.pallas_call(
        functools.partial(outputs_kernel, replicas=replicas),
        out_shape=(
            jax.ShapeDtypeStruct((layers, share, width), BF16),
            jax.ShapeDtypeStruct((layers, rows, width), BF16),
        ),
        grid=(layers, rows // step),
        in_specs=[
            pl.BlockSpec(right.shape, lambda l, d: (0, 0, 0)),
            pl.BlockSpec((1, rank, rank), lambda l, d: (l, 0, 0)),
            pl.BlockSpec((1, rank, step), lambda l, d: (l, 0, d)),
            pl.BlockSpec((1, rank, share), lambda l, d: (l, 0, 0)),
            pl.BlockSpec((1, step, width), lambda l, d: (l, d, 0)),
        ],
        out_specs=(
            pl.BlockSpec((1, share, width), lambda l, d: (l, 0, 0)),
            pl.BlockSpec((1, step, width), lambda l, d: (l, d, 0)),
        ),
        scratch_shapes=[pltpu.VMEM((2 * rank, width), BF16)],
        cost_estimate=cost(6e8, 15e6),
        name="outputs",
        compiler_params=room(50),
    )(right, inverse, left, own_left, moment)


def exchanged(x, axis):
    return lax.all_to_all(x, axis, 0, 0, tiled=True)


def body(context, out_grad, error_in, right_init):
    rank, rows = right_init.shape[1], out_grad.shape[2]
    core = lax.axis_index("tensor_1").astype(jnp.int32).reshape(1)
    grad_t = lax.all_gather(jnp.swapaxes(out_grad, 1, 2), TENSOR, axis=0, tiled=False)

    z = exchanged(sketch(right_init, context), TENSOR)
    error_part = error_sketch(right_init, error_in)
    send, keep = left_term(core, z, out_grad, error_part)
    swap = [(0, 1), (1, 0)]
    arrived = lax.ppermute(send, "tensor_1", swap)
    terms = exchanged(cut(keep, arrived, lax.axis_size(WIDE)), WIDE)
    own = exchanged(sum_copies(terms), WIDE)
    other = lax.ppermute(own, "tensor_1", swap)
    left = join(core, own, other, rank, rows)

    moment = moment_of(grad_t, context, error_in)
    replicas = lax.axis_size(DP)
    right = exchanged(right_term(left, moment, replicas), DP)
    right = exchanged(sum_copies(right), DP)
    inverse = inverse_of_gram(left)
    share = rows // replicas
    own_left = lax.dynamic_slice_in_dim(left, lax.axis_index(DP) * share, share, 2)
    return outputs(right, inverse, left, own_left, moment, replicas)


def solution(mesh):
    finer = Mesh(mesh.devices.reshape(4, 8, 4, 2), ("dp_0", "dp_1", "tensor_0", "tensor_1"))
    return jax.shard_map(
        body,
        mesh=finer,
        in_specs=(
            P(None, DP, TENSOR),
            P(None, DP_TENSOR, None),
            P(None, DP, TENSOR),
            P(None, None, TENSOR),
        ),
        out_specs=(P(None, DP, TENSOR), P(None, DP, TENSOR)),
        check_vma=False,
    )
```

```python
import functools

import jax
import jax.numpy as jnp
from jax import lax
from jax.experimental import pallas as pl
from jax.experimental.pallas import tpu as pltpu
from jax.sharding import Mesh
from jax.sharding import PartitionSpec as P


TENSOR = ("tensor_0", "tensor_1")
DP_TENSOR = ("dp_0", "dp_1", "tensor_0", "tensor_1")
DP = ("dp_0", "dp_1")
WIDE = ("dp_0", "dp_1", "tensor_0")
F32, BF16 = jnp.float32, jnp.bfloat16
HIGHEST = lax.Precision.HIGHEST
VMEM = pl.BlockSpec(memory_space=pltpu.VMEM)
SMEM = pl.BlockSpec(memory_space=pltpu.SMEM)


def room(mib):
    return pltpu.CompilerParams(vmem_limit_bytes=mib * 1024 * 1024)


def cost(flops, nbytes):
    return pl.CostEstimate(flops=int(flops), bytes_accessed=int(nbytes), transcendentals=0)


def two_parts(x):
    high = x.astype(BF16)
    return high, (x - high.astype(F32)).astype(BF16)


def dot(a, b, dims, **kw):
    return lax.dot_general(a, b, (dims, ((), ())), preferred_element_type=F32, **kw)


def sketch_kernel(r_ref, x_ref, o_ref):
    rank = r_ref.shape[1]
    for layer in range(r_ref.shape[0]):
        stacked = jnp.concatenate(two_parts(r_ref[layer]), axis=0)
        z = dot(stacked, x_ref[layer], ((1,), (1,)))
        z = (z[:rank] + z[rank:]).astype(BF16)
        for j in range(o_ref.shape[0]):
            o_ref[j, layer] = z[:, j * 128 : (j + 1) * 128]


def sketch(right_init, context):
    layers, rank, _ = right_init.shape
    tokens = context.shape[1]
    return pl.pallas_call(
        sketch_kernel,
        out_shape=jax.ShapeDtypeStruct((tokens // 128, layers, rank, 128), BF16),
        in_specs=[VMEM, VMEM],
        out_specs=VMEM,
        cost_estimate=cost(4e8, 2e6),
        name="sketch",
        compiler_params=room(56),
    )(right_init, context)


def error_sketch_kernel(r_ref, e_ref, o_ref):
    rank = r_ref.shape[1]
    stacked = jnp.concatenate(two_parts(r_ref[0]), axis=0)
    z = dot(stacked, e_ref[0], ((1,), (1,)))
    o_ref[0] = z[:rank] + z[rank:]


def error_sketch(right_init, error_in):
    layers, rank, width = right_init.shape
    rows = error_in.shape[1]
    step = 768
    return pl.pallas_call(
        error_sketch_kernel,
        out_shape=jax.ShapeDtypeStruct((layers, rank, rows), F32),
        grid=(layers, rows // step),
        in_specs=[
            pl.BlockSpec((1, rank, width), lambda l, d: (l, 0, 0)),
            pl.BlockSpec((1, step, width), lambda l, d: (l, d, 0)),
        ],
        out_specs=pl.BlockSpec((1, rank, step), lambda l, d: (l, 0, d)),
        cost_estimate=cost(6e8, 7e6),
        name="error_sketch",
        compiler_params=room(6),
    )(right_init, error_in)


def left_term_kernel(core_ref, z_ref, y_ref, e_ref, send_ref, keep_ref):
    rank = z_ref.shape[2]
    core = core_ref[0]
    for which, out in ((1 - core, send_ref), (core, keep_ref)):
        z = z_ref[0, which].astype(F32)
        for j in range(1, z_ref.shape[0]):
            z = z + z_ref[j, which].astype(F32)
        t = dot(jnp.concatenate(two_parts(z), axis=0), y_ref[which], ((1,), (0,)))
        out[...] = t[:rank] + t[rank:] + e_ref[which]


def left_term(core, z, own_grad, error_part):
    rank, rows = error_part.shape[1:]
    shape = jax.ShapeDtypeStruct((rank, rows), F32)
    return pl.pallas_call(
        left_term_kernel,
        out_shape=(shape, shape),
        in_specs=[SMEM, VMEM, VMEM, VMEM],
        out_specs=(VMEM, VMEM),
        cost_estimate=cost(2e8, 5e6),
        name="left_term",
        compiler_params=room(12),
    )(core, z, own_grad, error_part)


def cut_kernel(a_ref, b_ref, o_ref):
    bands, lanes = a_ref.shape[0] // 16, a_ref.shape[1] // 128
    for i in range(bands):
        for j in range(lanes):
            rows, cols = slice(i * 16, i * 16 + 16), slice(j * 128, j * 128 + 128)
            both = a_ref[rows, cols] + b_ref[rows, cols]
            o_ref[i * lanes + j] = both.astype(BF16)
    for p in range(bands * lanes, o_ref.shape[0]):
        o_ref[p] = jnp.zeros(o_ref.shape[1:], BF16)


def cut(a, b, pieces):
    return pl.pallas_call(
        cut_kernel,
        out_shape=jax.ShapeDtypeStruct((pieces, 16, 128), BF16),
        in_specs=[VMEM, VMEM],
        out_specs=VMEM,
        cost_estimate=cost(4e5, 1.2e6),
        name="cut",
        compiler_params=room(4),
    )(a, b)


def sum_copies_kernel(x_ref, o_ref):
    parts = [x_ref[p].astype(F32) for p in range(4)]
    for p in range(4, x_ref.shape[0], 4):
        for q in range(4):
            parts[q] = parts[q] + x_ref[p + q].astype(F32)
    total = ((parts[0] + parts[1]) + (parts[2] + parts[3])).astype(o_ref.dtype)
    for p in range(o_ref.shape[0]):
        o_ref[p] = total


def sum_copies(x, dtype):
    return pl.pallas_call(
        sum_copies_kernel,
        out_shape=jax.ShapeDtypeStruct(x.shape, dtype),
        in_specs=[VMEM],
        out_specs=VMEM,
        cost_estimate=cost(x.size, x.size * 4),
        name="sum_copies",
        compiler_params=room(4),
    )(x)


def own_tokens_kernel(core_ref, a_ref, b_ref, y_ref, l_ref, o_ref):
    core = core_ref[0]
    count, lanes = l_ref.shape[1] // 16, l_ref.shape[2] // 128
    for which, ref in ((core, a_ref), (1 - core, b_ref)):
        rows = [jnp.concatenate([ref[i * lanes + j] for j in range(lanes)], axis=1) for i in range(count)]
        left = jnp.concatenate(rows, axis=0)
        l_ref[which] = left
        w = dot(left, y_ref[which], ((1,), (1,))).astype(BF16)
        for k in range(o_ref.shape[0]):
            o_ref[k, which] = w


def own_tokens(core, own, other, own_grad, rank, count):
    rows = own_grad.shape[2]
    return pl.pallas_call(
        own_tokens_kernel,
        out_shape=(
            jax.ShapeDtypeStruct((2, rank, rows), BF16),
            jax.ShapeDtypeStruct((count, 2, rank, 128), BF16),
        ),
        in_specs=[SMEM, VMEM, VMEM, VMEM],
        out_specs=(VMEM, VMEM),
        cost_estimate=cost(2e8, 4e6),
        name="own_tokens",
        compiler_params=room(6),
    )(core, own, other, own_grad)


def left_error_kernel(l_ref, e_ref, o_ref):
    for layer in range(l_ref.shape[0]):
        o_ref[layer] = dot(l_ref[layer], e_ref[layer], ((1,), (0,)))


def left_error(left, error_in):
    layers, rank, _ = left.shape
    return pl.pallas_call(
        left_error_kernel,
        out_shape=jax.ShapeDtypeStruct((layers, rank, error_in.shape[2]), F32),
        in_specs=[VMEM, VMEM],
        out_specs=VMEM,
        cost_estimate=cost(6e8, 6e6),
        name="left_error",
        compiler_params=room(10),
    )(left, error_in)


def right_term_kernel(w_ref, x_ref, e_ref, o_ref):
    layers, rank, width = e_ref.shape
    count, lanes = rank // 16, width // 128
    for layer in range(layers):
        w = jnp.concatenate([w_ref[k, layer] for k in range(w_ref.shape[0])], axis=1)
        right = dot(w, x_ref[layer], ((1,), (0,))) + e_ref[layer]
        for i in range(count):
            for j in range(lanes):
                o_ref[(layer * count + i) * lanes + j] = right[i * 16 : i * 16 + 16, j * 128 : j * 128 + 128]
    for p in range(layers * count * lanes, o_ref.shape[0]):
        o_ref[p] = jnp.zeros(o_ref.shape[1:], o_ref.dtype)


def right_term(w, context, error_part, pieces):
    return pl.pallas_call(
        right_term_kernel,
        out_shape=jax.ShapeDtypeStruct((pieces, 16, 128), F32),
        in_specs=[VMEM, VMEM, VMEM],
        out_specs=VMEM,
        cost_estimate=cost(2e8, 3e6),
        name="right_term",
        compiler_params=room(6),
    )(w, context, error_part)


def turn_kernel(y_ref, *o_refs):
    for layer, o_ref in enumerate(o_refs):
        o_ref[...] = y_ref[layer].T


def turn(own_grad):
    layers, tokens, rows = own_grad.shape
    return pl.pallas_call(
        turn_kernel,
        out_shape=[jax.ShapeDtypeStruct((rows, tokens), BF16)] * layers,
        in_specs=[VMEM],
        out_specs=[VMEM] * layers,
        cost_estimate=cost(1e8, 3e6),
        name="turn",
        compiler_params=room(8),
    )(own_grad)


def moment_kernel(y_ref, x_ref, e_ref, o_ref):
    y = jnp.concatenate([y_ref[k] for k in range(y_ref.shape[0])], axis=1)
    o_ref[...] = dot(y, x_ref[0], ((1,), (0,))) + e_ref[0].astype(F32)


def moment_of(grad_t, context, error_in, layer):
    blocks, rows, _ = grad_t.shape
    tokens, width = context.shape[1:]
    step = 512
    return pl.pallas_call(
        moment_kernel,
        out_shape=jax.ShapeDtypeStruct((rows, width), F32),
        grid=(rows // step,),
        in_specs=[
            pl.BlockSpec((blocks, step, 128), lambda d: (0, d, 0)),
            pl.BlockSpec((1, tokens, width), lambda d: (layer, 0, 0)),
            pl.BlockSpec((1, step, width), lambda d: (layer, d, 0)),
        ],
        out_specs=pl.BlockSpec((step, width), lambda d: (d, 0)),
        cost_estimate=cost(4e9, 14e6),
        compiler_params=room(56),
    )(grad_t, context, error_in)


def inverse_kernel(l_ref, o_ref, t_ref):
    rank = l_ref.shape[1]
    row = lax.broadcasted_iota(jnp.int32, (rank, 2 * rank), 0)
    col = lax.broadcasted_iota(jnp.int32, (rank, 2 * rank), 1)
    work = []
    for layer in range(l_ref.shape[0]):
        left = l_ref[layer]
        turned = left.T
        t_ref[layer] = jnp.concatenate([turned, turned], axis=1)
        gram = dot(left, left, ((1,), (1,)))
        wide = jnp.concatenate([gram, jnp.zeros((rank, rank), F32)], axis=1)
        diag = jnp.sum(jnp.where(row == col, wide, 0.0), axis=1, keepdims=True)
        ridge = 1e-6 * (jnp.sum(diag, axis=0, keepdims=True) / rank)
        wide = wide + jnp.where(row == col, ridge, 0.0)
        work.append(jnp.where(col == row + rank, 1.0, wide))
    for k in range(rank):
        for layer in range(len(work)):
            a = work[layer]
            pivot_row = a[k : k + 1, :] / a[k : k + 1, k : k + 1]
            column = a[:, k : k + 1]
            work[layer] = jnp.where(row == k, pivot_row, a - column * pivot_row)
    for layer in range(len(work)):
        o_ref[layer] = work[layer][:, rank:]


def inverse_of_gram(left):
    layers, rank, rows = left.shape
    return pl.pallas_call(
        inverse_kernel,
        out_shape=(
            jax.ShapeDtypeStruct((layers, rank, rank), F32),
            jax.ShapeDtypeStruct((layers, rows, 2 * rank), BF16),
        ),
        in_specs=[VMEM],
        out_specs=(VMEM, VMEM),
        cost_estimate=cost(5e9, 2e6),
        name="gram_inverse",
        compiler_params=room(6),
    )(left)


def outputs_kernel(r_ref, g_ref, t_ref, own_ref, m0_ref, m1_ref, s_ref, e_ref, q_ref, *, replicas):
    layer, d = pl.program_id(0), pl.program_id(1)
    rank, width = g_ref.shape[1], m0_ref.shape[1]
    count, lanes = rank // 16, width // 128

    @pl.when(d == 0)
    def _():
        rows = [
            jnp.concatenate([r_ref[(layer * count + i) * lanes + j] for j in range(lanes)], axis=1)
            for i in range(count)
        ]
        q = dot(g_ref[0], jnp.concatenate(rows, axis=0), ((1,), (0,)), precision=HIGHEST)
        own = own_ref[0]
        s = dot(jnp.concatenate([own, own], axis=0), jnp.concatenate(two_parts(q), axis=0), ((0,), (0,)))
        s_ref[0] = s.astype(BF16)
        q_ref[...] = jnp.concatenate(two_parts(q * (-1.0 / replicas)), axis=0)

    update = dot(t_ref[0], q_ref[...], ((1,), (0,)))
    for which, m_ref in ((0, m0_ref), (1, m1_ref)):

        @pl.when(layer == which)
        def _():
            e_ref[0] = (m_ref[...] + update).astype(BF16)


def outputs(right, inverse, turned, own_left, moments, replicas):
    rows, width = moments[0].shape
    layers, rank, share = own_left.shape
    step = 768
    last = rows // step - 1
    return pl.pallas_call(
        functools.partial(outputs_kernel, replicas=replicas),
        out_shape=(
            jax.ShapeDtypeStruct((layers, share, width), BF16),
            jax.ShapeDtypeStruct((layers, rows, width), BF16),
        ),
        grid=(layers, rows // step),
        in_specs=[
            pl.BlockSpec(right.shape, lambda l, d: (0, 0, 0)),
            pl.BlockSpec((1, rank, rank), lambda l, d: (l, 0, 0)),
            pl.BlockSpec((1, step, 2 * rank), lambda l, d: (l, d, 0)),
            pl.BlockSpec((1, rank, share), lambda l, d: (l, 0, 0)),
            pl.BlockSpec((step, width), lambda l, d: (d * (1 - l) + last * l, 0)),
            pl.BlockSpec((step, width), lambda l, d: (d * l, 0)),
        ],
        out_specs=(
            pl.BlockSpec((1, share, width), lambda l, d: (l, 0, 0)),
            pl.BlockSpec((1, step, width), lambda l, d: (l, d, 0)),
        ),
        scratch_shapes=[pltpu.VMEM((2 * rank, width), BF16)],
        cost_estimate=cost(6e8, 15e6),
        name="outputs",
        compiler_params=room(50),
    )(right, inverse, turned, own_left, *moments)


def exchanged(x, axis):
    return lax.all_to_all(x, axis, 0, 0, tiled=True)


SWAP = [(0, 1), (1, 0)]


def swapped(x):
    return lax.ppermute(x, "tensor_1", SWAP)


def body(context, out_grad, error_in, right_init):
    rank, rows = right_init.shape[1], out_grad.shape[2]
    replicas = lax.axis_size(DP)
    core = lax.axis_index("tensor_1").astype(jnp.int32).reshape(1)
    z = exchanged(sketch(right_init, context), TENSOR)
    grads = []
    for turned in turn(out_grad):
        grads.append(lax.all_gather(turned, TENSOR, axis=0, tiled=False))
    error_part = error_sketch(right_init, error_in)
    send, keep = left_term(core, z, out_grad, error_part)
    arrived = swapped(send)
    terms = exchanged(cut(keep, arrived, lax.axis_size(WIDE)), WIDE)
    own = exchanged(sum_copies(terms, BF16), WIDE)
    other = swapped(own)
    left, w = own_tokens(core, own, other, out_grad, rank, lax.axis_size(TENSOR))
    w = exchanged(w, TENSOR)
    right = right_term(w, context, left_error(left, error_in), replicas)
    right = exchanged(right, DP)
    right = exchanged(sum_copies(right, F32), DP)
    inverse, turned = inverse_of_gram(left)
    moments = []
    for layer, grad_t in enumerate(grads):
        moments.append(moment_of(grad_t, context, error_in, layer))
    share = rows // replicas
    own_left = lax.dynamic_slice_in_dim(left, lax.axis_index(DP) * share, share, 2)
    return outputs(right, inverse, turned, own_left, moments, replicas)


def solution(mesh):
    finer = Mesh(mesh.devices.reshape(4, 8, 4, 2), ("dp_0", "dp_1", "tensor_0", "tensor_1"))
    return jax.shard_map(
        body,
        mesh=finer,
        in_specs=(
            P(None, DP, TENSOR),
            P(None, DP_TENSOR, None),
            P(None, DP, TENSOR),
            P(None, None, TENSOR),
        ),
        out_specs=(P(None, DP, TENSOR), P(None, DP, TENSOR)),
        check_vma=False,
    )
```

```python
import functools

import jax
import jax.numpy as jnp
from jax import lax
from jax.experimental import pallas as pl
from jax.experimental.pallas import tpu as pltpu
from jax.sharding import Mesh
from jax.sharding import PartitionSpec as P


TENSOR = ("tensor_0", "tensor_1")
DP_TENSOR = ("dp_0", "dp_1", "tensor_0", "tensor_1")
DP = ("dp_0", "dp_1")
WIDE = ("dp_0", "dp_1", "tensor_0")
F32, BF16 = jnp.float32, jnp.bfloat16
HIGHEST = lax.Precision.HIGHEST
VMEM = pl.BlockSpec(memory_space=pltpu.VMEM)
SMEM = pl.BlockSpec(memory_space=pltpu.SMEM)


def room(mib):
    return pltpu.CompilerParams(vmem_limit_bytes=mib * 1024 * 1024)


def cost(flops, nbytes):
    return pl.CostEstimate(flops=int(flops), bytes_accessed=int(nbytes), transcendentals=0)


def two_parts(x):
    high = x.astype(BF16)
    return high, (x - high.astype(F32)).astype(BF16)


def dot(a, b, dims, **kw):
    return lax.dot_general(a, b, (dims, ((), ())), preferred_element_type=F32, **kw)


def sketch_kernel(r_ref, x_ref, o_ref):
    rank = r_ref.shape[1]
    for layer in range(r_ref.shape[0]):
        stacked = jnp.concatenate(two_parts(r_ref[layer]), axis=0)
        z = dot(stacked, x_ref[layer], ((1,), (1,)))
        z = (z[:rank] + z[rank:]).astype(BF16)
        for j in range(o_ref.shape[0]):
            o_ref[j, layer] = z[:, j * 128 : (j + 1) * 128]


def sketch(right_init, context):
    layers, rank, _ = right_init.shape
    tokens = context.shape[1]
    return pl.pallas_call(
        sketch_kernel,
        out_shape=jax.ShapeDtypeStruct((tokens // 128, layers, rank, 128), BF16),
        in_specs=[VMEM, VMEM],
        out_specs=VMEM,
        cost_estimate=cost(4e8, 2e6),
        name="sketch",
        compiler_params=room(56),
    )(right_init, context)


def error_sketch_kernel(r_ref, e_ref, o_ref):
    rank = r_ref.shape[1]
    stacked = jnp.concatenate(two_parts(r_ref[0]), axis=0)
    z = dot(stacked, e_ref[0], ((1,), (1,)))
    o_ref[0] = z[:rank] + z[rank:]


def error_sketch(right_init, error_in):
    layers, rank, width = right_init.shape
    rows = error_in.shape[1]
    step = 768
    return pl.pallas_call(
        error_sketch_kernel,
        out_shape=jax.ShapeDtypeStruct((layers, rank, rows), F32),
        grid=(layers, rows // step),
        in_specs=[
            pl.BlockSpec((1, rank, width), lambda l, d: (l, 0, 0)),
            pl.BlockSpec((1, step, width), lambda l, d: (l, d, 0)),
        ],
        out_specs=pl.BlockSpec((1, rank, step), lambda l, d: (l, 0, d)),
        cost_estimate=cost(6e8, 7e6),
        name="error_sketch",
        compiler_params=room(6),
    )(right_init, error_in)


def left_term_kernel(core_ref, z_ref, y_ref, e_ref, send_ref, keep_ref):
    rank = z_ref.shape[2]
    core = core_ref[0]
    for which, out in ((1 - core, send_ref), (core, keep_ref)):
        z = z_ref[0, which].astype(F32)
        for j in range(1, z_ref.shape[0]):
            z = z + z_ref[j, which].astype(F32)
        t = dot(jnp.concatenate(two_parts(z), axis=0), y_ref[which], ((1,), (0,)))
        out[...] = t[:rank] + t[rank:] + e_ref[which]


def left_term(core, z, own_grad, error_part):
    rank, rows = error_part.shape[1:]
    shape = jax.ShapeDtypeStruct((rank, rows), F32)
    return pl.pallas_call(
        left_term_kernel,
        out_shape=(shape, shape),
        in_specs=[SMEM, VMEM, VMEM, VMEM],
        out_specs=(VMEM, VMEM),
        cost_estimate=cost(2e8, 5e6),
        name="left_term",
        compiler_params=room(12),
    )(core, z, own_grad, error_part)


def cut_kernel(a_ref, b_ref, o_ref):
    bands, lanes = a_ref.shape[0] // 16, a_ref.shape[1] // 128
    for i in range(bands):
        for j in range(lanes):
            rows, cols = slice(i * 16, i * 16 + 16), slice(j * 128, j * 128 + 128)
            both = a_ref[rows, cols] + b_ref[rows, cols]
            o_ref[i * lanes + j] = both.astype(BF16)
    for p in range(bands * lanes, o_ref.shape[0]):
        o_ref[p] = jnp.zeros(o_ref.shape[1:], BF16)


def cut(a, b, pieces):
    return pl.pallas_call(
        cut_kernel,
        out_shape=jax.ShapeDtypeStruct((pieces, 16, 128), BF16),
        in_specs=[VMEM, VMEM],
        out_specs=VMEM,
        cost_estimate=cost(4e5, 1.2e6),
        name="cut",
        compiler_params=room(4),
    )(a, b)


def sum_copies_kernel(x_ref, o_ref):
    parts = [x_ref[p].astype(F32) for p in range(4)]
    for p in range(4, x_ref.shape[0], 4):
        for q in range(4):
            parts[q] = parts[q] + x_ref[p + q].astype(F32)
    total = ((parts[0] + parts[1]) + (parts[2] + parts[3])).astype(o_ref.dtype)
    for p in range(o_ref.shape[0]):
        o_ref[p] = total


def sum_copies(x, dtype):
    return pl.pallas_call(
        sum_copies_kernel,
        out_shape=jax.ShapeDtypeStruct(x.shape, dtype),
        in_specs=[VMEM],
        out_specs=VMEM,
        cost_estimate=cost(x.size, x.size * 4),
        name="sum_copies",
        compiler_params=room(4),
    )(x)


def own_tokens_kernel(core_ref, a_ref, b_ref, y_ref, l_ref, o_ref):
    core = core_ref[0]
    count, lanes = l_ref.shape[1] // 16, l_ref.shape[2] // 128
    for which, ref in ((core, a_ref), (1 - core, b_ref)):
        rows = [jnp.concatenate([ref[i * lanes + j] for j in range(lanes)], axis=1) for i in range(count)]
        left = jnp.concatenate(rows, axis=0)
        l_ref[which] = left
        w = dot(left, y_ref[which], ((1,), (1,))).astype(BF16)
        for k in range(o_ref.shape[0]):
            o_ref[k, which] = w


def own_tokens(core, own, other, own_grad, rank, count):
    rows = own_grad.shape[2]
    return pl.pallas_call(
        own_tokens_kernel,
        out_shape=(
            jax.ShapeDtypeStruct((2, rank, rows), BF16),
            jax.ShapeDtypeStruct((count, 2, rank, 128), BF16),
        ),
        in_specs=[SMEM, VMEM, VMEM, VMEM],
        out_specs=(VMEM, VMEM),
        cost_estimate=cost(2e8, 4e6),
        name="own_tokens",
        compiler_params=room(6),
    )(core, own, other, own_grad)


def left_error_kernel(l_ref, e_ref, o_ref):
    for layer in range(l_ref.shape[0]):
        o_ref[layer] = dot(l_ref[layer], e_ref[layer], ((1,), (0,)))


def left_error(left, error_in):
    layers, rank, _ = left.shape
    return pl.pallas_call(
        left_error_kernel,
        out_shape=jax.ShapeDtypeStruct((layers, rank, error_in.shape[2]), F32),
        in_specs=[VMEM, VMEM],
        out_specs=VMEM,
        cost_estimate=cost(6e8, 6e6),
        name="left_error",
        compiler_params=room(10),
    )(left, error_in)


def right_term_kernel(w_ref, x_ref, e_ref, o_ref):
    layers, rank, width = e_ref.shape
    count, lanes = rank // 16, width // 128
    for layer in range(layers):
        w = jnp.concatenate([w_ref[k, layer] for k in range(w_ref.shape[0])], axis=1)
        right = dot(w, x_ref[layer], ((1,), (0,))) + e_ref[layer]
        for i in range(count):
            for j in range(lanes):
                o_ref[(layer * count + i) * lanes + j] = right[i * 16 : i * 16 + 16, j * 128 : j * 128 + 128]
    for p in range(layers * count * lanes, o_ref.shape[0]):
        o_ref[p] = jnp.zeros(o_ref.shape[1:], o_ref.dtype)


def right_term(w, context, error_part, pieces):
    return pl.pallas_call(
        right_term_kernel,
        out_shape=jax.ShapeDtypeStruct((pieces, 16, 128), F32),
        in_specs=[VMEM, VMEM, VMEM],
        out_specs=VMEM,
        cost_estimate=cost(2e8, 3e6),
        name="right_term",
        compiler_params=room(6),
    )(w, context, error_part)


def turn_kernel(y_ref, *o_refs):
    for layer, o_ref in enumerate(o_refs):
        o_ref[...] = y_ref[layer].T


def turn(own_grad):
    layers, tokens, rows = own_grad.shape
    return pl.pallas_call(
        turn_kernel,
        out_shape=[jax.ShapeDtypeStruct((rows, tokens), BF16)] * layers,
        in_specs=[VMEM],
        out_specs=[VMEM] * layers,
        cost_estimate=cost(1e8, 3e6),
        name="turn",
        compiler_params=room(8),
    )(own_grad)


def moment_kernel(y_ref, x_ref, e_ref, o_ref):
    y = jnp.concatenate([y_ref[k] for k in range(y_ref.shape[0])], axis=1)
    o_ref[...] = (dot(y, x_ref[0], ((1,), (0,))) + e_ref[0].astype(F32)).astype(BF16)


def moment_of(grad_t, context, error_in, layer):
    blocks, rows, _ = grad_t.shape
    tokens, width = context.shape[1:]
    step = 512
    return pl.pallas_call(
        moment_kernel,
        out_shape=jax.ShapeDtypeStruct((rows, width), BF16),
        grid=(rows // step,),
        in_specs=[
            pl.BlockSpec((blocks, step, 128), lambda d: (0, d, 0)),
            pl.BlockSpec((1, tokens, width), lambda d: (layer, 0, 0)),
            pl.BlockSpec((1, step, width), lambda d: (layer, d, 0)),
        ],
        out_specs=pl.BlockSpec((step, width), lambda d: (d, 0)),
        cost_estimate=cost(4e9, 14e6),
        compiler_params=room(56),
    )(grad_t, context, error_in)


def inverse_kernel(l_ref, o_ref, t_ref):
    rank = l_ref.shape[1]
    row = lax.broadcasted_iota(jnp.int32, (rank, 2 * rank), 0)
    col = lax.broadcasted_iota(jnp.int32, (rank, 2 * rank), 1)
    work = []
    for layer in range(l_ref.shape[0]):
        left = l_ref[layer]
        turned = left.T
        t_ref[layer] = jnp.concatenate([turned, turned], axis=1)
        gram = dot(left, left, ((1,), (1,)))
        wide = jnp.concatenate([gram, jnp.zeros((rank, rank), F32)], axis=1)
        diag = jnp.sum(jnp.where(row == col, wide, 0.0), axis=1, keepdims=True)
        ridge = 1e-6 * (jnp.sum(diag, axis=0, keepdims=True) / rank)
        wide = wide + jnp.where(row == col, ridge, 0.0)
        work.append(jnp.where(col == row + rank, 1.0, wide))
    for k in range(rank):
        for layer in range(len(work)):
            a = work[layer]
            pivot_row = a[k : k + 1, :] / a[k : k + 1, k : k + 1]
            column = a[:, k : k + 1]
            work[layer] = jnp.where(row == k, pivot_row, a - column * pivot_row)
    for layer in range(len(work)):
        o_ref[layer] = work[layer][:, rank:]


def inverse_of_gram(left):
    layers, rank, rows = left.shape
    return pl.pallas_call(
        inverse_kernel,
        out_shape=(
            jax.ShapeDtypeStruct((layers, rank, rank), F32),
            jax.ShapeDtypeStruct((layers, rows, 2 * rank), BF16),
        ),
        in_specs=[VMEM],
        out_specs=(VMEM, VMEM),
        cost_estimate=cost(5e9, 2e6),
        name="gram_inverse",
        compiler_params=room(6),
    )(left)


def outputs_kernel(r_ref, g_ref, t_ref, own_ref, m0_ref, m1_ref, s_ref, e_ref, q_ref, *, replicas):
    layer, d = pl.program_id(0), pl.program_id(1)
    rank, width = g_ref.shape[1], m0_ref.shape[1]
    count, lanes = rank // 16, width // 128

    @pl.when(d == 0)
    def _():
        rows = [
            jnp.concatenate([r_ref[(layer * count + i) * lanes + j] for j in range(lanes)], axis=1)
            for i in range(count)
        ]
        q = dot(g_ref[0], jnp.concatenate(rows, axis=0), ((1,), (0,)), precision=HIGHEST)
        own = own_ref[0]
        s = dot(jnp.concatenate([own, own], axis=0), jnp.concatenate(two_parts(q), axis=0), ((0,), (0,)))
        s_ref[0] = s.astype(BF16)
        q_ref[...] = jnp.concatenate(two_parts(q * (-1.0 / replicas)), axis=0)

    update = dot(t_ref[0], q_ref[...], ((1,), (0,)))
    for which, m_ref in ((0, m0_ref), (1, m1_ref)):

        @pl.when(layer == which)
        def _():
            e_ref[0] = (m_ref[...].astype(F32) + update).astype(BF16)


def outputs(right, inverse, turned, own_left, moments, replicas):
    rows, width = moments[0].shape
    layers, rank, share = own_left.shape
    step = 768
    last = rows // step - 1
    return pl.pallas_call(
        functools.partial(outputs_kernel, replicas=replicas),
        out_shape=(
            jax.ShapeDtypeStruct((layers, share, width), BF16),
            jax.ShapeDtypeStruct((layers, rows, width), BF16),
        ),
        grid=(layers, rows // step),
        in_specs=[
            pl.BlockSpec(right.shape, lambda l, d: (0, 0, 0)),
            pl.BlockSpec((1, rank, rank), lambda l, d: (l, 0, 0)),
            pl.BlockSpec((1, step, 2 * rank), lambda l, d: (l, d, 0)),
            pl.BlockSpec((1, rank, share), lambda l, d: (l, 0, 0)),
            pl.BlockSpec((step, width), lambda l, d: (d * (1 - l) + last * l, 0)),
            pl.BlockSpec((step, width), lambda l, d: (d * l, 0)),
        ],
        out_specs=(
            pl.BlockSpec((1, share, width), lambda l, d: (l, 0, 0)),
            pl.BlockSpec((1, step, width), lambda l, d: (l, d, 0)),
        ),
        scratch_shapes=[pltpu.VMEM((2 * rank, width), BF16)],
        cost_estimate=cost(6e8, 15e6),
        name="outputs",
        compiler_params=room(50),
    )(right, inverse, turned, own_left, *moments)


def exchanged(x, axis):
    return lax.all_to_all(x, axis, 0, 0, tiled=True)


SWAP = [(0, 1), (1, 0)]


def swapped(x):
    return lax.ppermute(x, "tensor_1", SWAP)


def body(context, out_grad, error_in, right_init):
    rank, rows = right_init.shape[1], out_grad.shape[2]
    replicas = lax.axis_size(DP)
    core = lax.axis_index("tensor_1").astype(jnp.int32).reshape(1)
    z = exchanged(sketch(right_init, context), TENSOR)
    grads = []
    turns = turn(out_grad)
    for turned in turns:
        grads.append(lax.all_gather(turned, TENSOR, axis=0, tiled=False))
    error_part = error_sketch(right_init, error_in)
    send, keep = left_term(core, z, out_grad, error_part)
    arrived = swapped(send)
    terms = exchanged(cut(keep, arrived, lax.axis_size(WIDE)), WIDE)
    own = exchanged(sum_copies(terms, BF16), WIDE)
    other = swapped(own)
    left, w = own_tokens(core, own, other, out_grad, rank, lax.axis_size(TENSOR))
    w = exchanged(w, TENSOR)
    right = right_term(w, context, left_error(left, error_in), replicas)
    right = exchanged(right, DP)
    right = exchanged(sum_copies(right, F32), DP)
    inverse, turned = inverse_of_gram(left)
    moments = []
    for layer, grad_t in enumerate(grads):
        moments.append(moment_of(grad_t, context, error_in, layer))
    share = rows // replicas
    own_left = lax.dynamic_slice_in_dim(left, lax.axis_index(DP) * share, share, 2)
    return outputs(right, inverse, turned, own_left, moments, replicas)


def solution(mesh):
    finer = Mesh(mesh.devices.reshape(4, 8, 4, 2), ("dp_0", "dp_1", "tensor_0", "tensor_1"))
    return jax.shard_map(
        body,
        mesh=finer,
        in_specs=(
            P(None, DP, TENSOR),
            P(None, DP_TENSOR, None),
            P(None, DP, TENSOR),
            P(None, None, TENSOR),
        ),
        out_specs=(P(None, DP, TENSOR), P(None, DP, TENSOR)),
        check_vma=False,
    )
```

```python
import functools

import jax
import jax.numpy as jnp
from jax import lax
from jax.experimental import pallas as pl
from jax.experimental.pallas import tpu as pltpu
from jax.sharding import Mesh
from jax.sharding import PartitionSpec as P


TENSOR = ("tensor_0", "tensor_1")
DP_TENSOR = ("dp_0", "dp_1", "tensor_0", "tensor_1")
DP = ("dp_0", "dp_1")
WIDE = ("dp_0", "dp_1", "tensor_0")
F32, BF16 = jnp.float32, jnp.bfloat16
HIGHEST = lax.Precision.HIGHEST
VMEM = pl.BlockSpec(memory_space=pltpu.VMEM)
SMEM = pl.BlockSpec(memory_space=pltpu.SMEM)


def room(mib):
    return pltpu.CompilerParams(vmem_limit_bytes=mib * 1024 * 1024)


def cost(flops, nbytes):
    return pl.CostEstimate(flops=int(flops), bytes_accessed=int(nbytes), transcendentals=0)


def two_parts(x):
    high = x.astype(BF16)
    return high, (x - high.astype(F32)).astype(BF16)


def dot(a, b, dims, **kw):
    return lax.dot_general(a, b, (dims, ((), ())), preferred_element_type=F32, **kw)


def sketch_kernel(r_ref, x_ref, o_ref):
    rank = r_ref.shape[1]
    for layer in range(r_ref.shape[0]):
        stacked = jnp.concatenate(two_parts(r_ref[layer]), axis=0)
        z = dot(stacked, x_ref[layer], ((1,), (1,)))
        z = (z[:rank] + z[rank:]).astype(BF16)
        for j in range(o_ref.shape[0]):
            o_ref[j, layer] = z[:, j * 128 : (j + 1) * 128]


def sketch(right_init, context):
    layers, rank, _ = right_init.shape
    tokens = context.shape[1]
    return pl.pallas_call(
        sketch_kernel,
        out_shape=jax.ShapeDtypeStruct((tokens // 128, layers, rank, 128), BF16),
        in_specs=[VMEM, VMEM],
        out_specs=VMEM,
        cost_estimate=cost(4e8, 2e6),
        name="sketch",
        compiler_params=room(56),
    )(right_init, context)


def error_sketch_kernel(r_ref, e_ref, o_ref):
    rank = r_ref.shape[1]
    stacked = jnp.concatenate(two_parts(r_ref[0]), axis=0)
    z = dot(stacked, e_ref[0], ((1,), (1,)))
    o_ref[0] = z[:rank] + z[rank:]


def error_sketch(right_init, error_in):
    layers, rank, width = right_init.shape
    rows = error_in.shape[1]
    step = 768
    return pl.pallas_call(
        error_sketch_kernel,
        out_shape=jax.ShapeDtypeStruct((layers, rank, rows), F32),
        grid=(layers, rows // step),
        in_specs=[
            pl.BlockSpec((1, rank, width), lambda l, d: (l, 0, 0)),
            pl.BlockSpec((1, step, width), lambda l, d: (l, d, 0)),
        ],
        out_specs=pl.BlockSpec((1, rank, step), lambda l, d: (l, 0, d)),
        cost_estimate=cost(6e8, 7e6),
        name="error_sketch",
        compiler_params=room(6),
    )(right_init, error_in)


def left_term_kernel(core_ref, z_ref, y_ref, e_ref, send_ref, keep_ref):
    rank = z_ref.shape[2]
    core = core_ref[0]
    for which, out in ((1 - core, send_ref), (core, keep_ref)):
        z = z_ref[0, which].astype(F32)
        for j in range(1, z_ref.shape[0]):
            z = z + z_ref[j, which].astype(F32)
        t = dot(jnp.concatenate(two_parts(z), axis=0), y_ref[which], ((1,), (0,)))
        out[...] = t[:rank] + t[rank:] + e_ref[which]


def left_term(core, z, own_grad, error_part):
    rank, rows = error_part.shape[1:]
    shape = jax.ShapeDtypeStruct((rank, rows), F32)
    return pl.pallas_call(
        left_term_kernel,
        out_shape=(shape, shape),
        in_specs=[SMEM, VMEM, VMEM, VMEM],
        out_specs=(VMEM, VMEM),
        cost_estimate=cost(2e8, 5e6),
        name="left_term",
        compiler_params=room(12),
    )(core, z, own_grad, error_part)


def cut_kernel(a_ref, b_ref, o_ref):
    high, wide = o_ref.shape[1:]
    across = a_ref.shape[1] // wide
    both = (a_ref[...] + b_ref[...]).astype(BF16)
    for p in range(o_ref.shape[0]):
        i, j = divmod(p, across)
        o_ref[p] = both[i * high : i * high + high, j * wide : j * wide + wide]


def cut(a, b, pieces):
    rank, rows = a.shape
    high, wide = 4, 384
    assert pieces * high * wide == rank * rows
    return pl.pallas_call(
        cut_kernel,
        out_shape=jax.ShapeDtypeStruct((pieces, high, wide), BF16),
        in_specs=[VMEM, VMEM],
        out_specs=VMEM,
        cost_estimate=cost(4e5, 1.2e6),
        name="cut",
        compiler_params=room(6),
    )(a, b)


def sum_copies_kernel(x_ref, o_ref):
    parts = [x_ref[p].astype(F32) for p in range(4)]
    for p in range(4, x_ref.shape[0], 4):
        for q in range(4):
            parts[q] = parts[q] + x_ref[p + q].astype(F32)
    total = ((parts[0] + parts[1]) + (parts[2] + parts[3])).astype(o_ref.dtype)
    for p in range(o_ref.shape[0]):
        o_ref[p] = total


def sum_copies(x, dtype):
    return pl.pallas_call(
        sum_copies_kernel,
        out_shape=jax.ShapeDtypeStruct(x.shape, dtype),
        in_specs=[VMEM],
        out_specs=VMEM,
        cost_estimate=cost(x.size, x.size * 4),
        name="sum_copies",
        compiler_params=room(4),
    )(x)


def own_tokens_kernel(core_ref, a_ref, b_ref, y_ref, l_ref, o_ref):
    core = core_ref[0]
    high, wide = a_ref.shape[1:]
    across = l_ref.shape[2] // wide
    for which, ref in ((core, a_ref), (1 - core, b_ref)):
        rows = [
            jnp.concatenate([ref[i * across + j] for j in range(across)], axis=1)
            for i in range(l_ref.shape[1] // high)
        ]
        left = jnp.concatenate(rows, axis=0)
        l_ref[which] = left
        w = dot(left, y_ref[which], ((1,), (1,))).astype(BF16)
        for k in range(o_ref.shape[0]):
            o_ref[k, which] = w


def own_tokens(core, own, other, own_grad, rank, count):
    rows = own_grad.shape[2]
    return pl.pallas_call(
        own_tokens_kernel,
        out_shape=(
            jax.ShapeDtypeStruct((2, rank, rows), BF16),
            jax.ShapeDtypeStruct((count, 2, rank, 128), BF16),
        ),
        in_specs=[SMEM, VMEM, VMEM, VMEM],
        out_specs=(VMEM, VMEM),
        cost_estimate=cost(2e8, 4e6),
        name="own_tokens",
        compiler_params=room(6),
    )(core, own, other, own_grad)


def left_error_kernel(l_ref, e_ref, o_ref):
    for layer in range(l_ref.shape[0]):
        o_ref[layer] = dot(l_ref[layer], e_ref[layer], ((1,), (0,)))


def left_error(left, error_in):
    layers, rank, _ = left.shape
    return pl.pallas_call(
        left_error_kernel,
        out_shape=jax.ShapeDtypeStruct((layers, rank, error_in.shape[2]), F32),
        in_specs=[VMEM, VMEM],
        out_specs=VMEM,
        cost_estimate=cost(6e8, 6e6),
        name="left_error",
        compiler_params=room(10),
    )(left, error_in)


def right_term_kernel(w_ref, x_ref, e_ref, o_ref):
    layers, rank, width = e_ref.shape
    count, lanes = rank // 16, width // 128
    for layer in range(layers):
        w = jnp.concatenate([w_ref[k, layer] for k in range(w_ref.shape[0])], axis=1)
        right = dot(w, x_ref[layer], ((1,), (0,))) + e_ref[layer]
        for i in range(count):
            for j in range(lanes):
                o_ref[(layer * count + i) * lanes + j] = right[i * 16 : i * 16 + 16, j * 128 : j * 128 + 128]
    for p in range(layers * count * lanes, o_ref.shape[0]):
        o_ref[p] = jnp.zeros(o_ref.shape[1:], o_ref.dtype)


def right_term(w, context, error_part, pieces):
    return pl.pallas_call(
        right_term_kernel,
        out_shape=jax.ShapeDtypeStruct((pieces, 16, 128), F32),
        in_specs=[VMEM, VMEM, VMEM],
        out_specs=VMEM,
        cost_estimate=cost(2e8, 3e6),
        name="right_term",
        compiler_params=room(6),
    )(w, context, error_part)


def turn_kernel(y_ref, *o_refs):
    for layer, o_ref in enumerate(o_refs):
        o_ref[...] = y_ref[layer].T


def turn(own_grad):
    layers, tokens, rows = own_grad.shape
    return pl.pallas_call(
        turn_kernel,
        out_shape=[jax.ShapeDtypeStruct((rows, tokens), BF16)] * layers,
        in_specs=[VMEM],
        out_specs=[VMEM] * layers,
        cost_estimate=cost(1e8, 3e6),
        name="turn",
        compiler_params=room(8),
    )(own_grad)


def moment_kernel(y_ref, x_ref, e_ref, o_ref):
    y = jnp.concatenate([y_ref[k] for k in range(y_ref.shape[0])], axis=1)
    o_ref[...] = (dot(y, x_ref[0], ((1,), (0,))) + e_ref[0].astype(F32)).astype(BF16)


def moment_of(grad_t, context, error_in, layer):
    blocks, rows, _ = grad_t.shape
    tokens, width = context.shape[1:]
    step = 512
    return pl.pallas_call(
        moment_kernel,
        out_shape=jax.ShapeDtypeStruct((rows, width), BF16),
        grid=(rows // step,),
        in_specs=[
            pl.BlockSpec((blocks, step, 128), lambda d: (0, d, 0)),
            pl.BlockSpec((1, tokens, width), lambda d: (layer, 0, 0)),
            pl.BlockSpec((1, step, width), lambda d: (layer, d, 0)),
        ],
        out_specs=pl.BlockSpec((step, width), lambda d: (d, 0)),
        cost_estimate=cost(4e9, 14e6),
        compiler_params=room(56),
    )(grad_t, context, error_in)


def inverse_kernel(l_ref, o_ref, t_ref):
    rank = l_ref.shape[1]
    row = lax.broadcasted_iota(jnp.int32, (rank, 2 * rank), 0)
    col = lax.broadcasted_iota(jnp.int32, (rank, 2 * rank), 1)
    work = []
    for layer in range(l_ref.shape[0]):
        left = l_ref[layer]
        turned = left.T
        t_ref[layer] = jnp.concatenate([turned, turned], axis=1)
        gram = dot(left, left, ((1,), (1,)))
        wide = jnp.concatenate([gram, jnp.zeros((rank, rank), F32)], axis=1)
        diag = jnp.sum(jnp.where(row == col, wide, 0.0), axis=1, keepdims=True)
        ridge = 1e-6 * (jnp.sum(diag, axis=0, keepdims=True) / rank)
        wide = wide + jnp.where(row == col, ridge, 0.0)
        work.append(jnp.where(col == row + rank, 1.0, wide))
    for k in range(rank):
        for layer in range(len(work)):
            a = work[layer]
            pivot_row = a[k : k + 1, :] / a[k : k + 1, k : k + 1]
            column = a[:, k : k + 1]
            work[layer] = jnp.where(row == k, pivot_row, a - column * pivot_row)
    for layer in range(len(work)):
        o_ref[layer] = work[layer][:, rank:]


def inverse_of_gram(left):
    layers, rank, rows = left.shape
    return pl.pallas_call(
        inverse_kernel,
        out_shape=(
            jax.ShapeDtypeStruct((layers, rank, rank), F32),
            jax.ShapeDtypeStruct((layers, rows, 2 * rank), BF16),
        ),
        in_specs=[VMEM],
        out_specs=(VMEM, VMEM),
        cost_estimate=cost(5e9, 2e6),
        name="gram_inverse",
        compiler_params=room(6),
    )(left)


def outputs_kernel(r_ref, g_ref, t_ref, own_ref, m0_ref, m1_ref, s_ref, e_ref, q_ref, *, replicas):
    layer, d = pl.program_id(0), pl.program_id(1)
    rank, width = g_ref.shape[1], m0_ref.shape[1]
    count, lanes = rank // 16, width // 128

    @pl.when(d == 0)
    def _():
        rows = [
            jnp.concatenate([r_ref[(layer * count + i) * lanes + j] for j in range(lanes)], axis=1)
            for i in range(count)
        ]
        q = dot(g_ref[0], jnp.concatenate(rows, axis=0), ((1,), (0,)), precision=HIGHEST)
        own = own_ref[0]
        s = dot(jnp.concatenate([own, own], axis=0), jnp.concatenate(two_parts(q), axis=0), ((0,), (0,)))
        s_ref[0] = s.astype(BF16)
        q_ref[...] = jnp.concatenate(two_parts(q * (-1.0 / replicas)), axis=0)

    step = e_ref.shape[1]
    here = pl.ds(pl.multiple_of(d * step, step), step)
    update = dot(t_ref[layer, here, :], q_ref[...], ((1,), (0,)))
    for which, m_ref in ((0, m0_ref), (1, m1_ref)):

        @pl.when(layer == which)
        def _():
            e_ref[0] = (m_ref[here, :].astype(F32) + update).astype(BF16)


def outputs(right, inverse, turned, own_left, moments, replicas):
    rows, width = moments[0].shape
    layers, rank, share = own_left.shape
    step = 768
    return pl.pallas_call(
        functools.partial(outputs_kernel, replicas=replicas),
        out_shape=(
            jax.ShapeDtypeStruct((layers, share, width), BF16),
            jax.ShapeDtypeStruct((layers, rows, width), BF16),
        ),
        grid=(layers, rows // step),
        in_specs=[
            pl.BlockSpec(right.shape, lambda l, d: (0, 0, 0)),
            pl.BlockSpec((1, rank, rank), lambda l, d: (l, 0, 0)),
            VMEM,
            pl.BlockSpec((1, rank, share), lambda l, d: (l, 0, 0)),
            VMEM,
            VMEM,
        ],
        out_specs=(
            pl.BlockSpec((1, share, width), lambda l, d: (l, 0, 0)),
            pl.BlockSpec((1, step, width), lambda l, d: (l, d, 0)),
        ),
        scratch_shapes=[pltpu.VMEM((2 * rank, width), BF16)],
        cost_estimate=cost(6e8, 15e6),
        name="outputs",
        compiler_params=room(14),
    )(right, inverse, turned, own_left, *moments)


def exchanged(x, axis):
    return lax.all_to_all(x, axis, 0, 0, tiled=True)


SWAP = [(0, 1), (1, 0)]


def swapped(x):
    return lax.ppermute(x, "tensor_1", SWAP)


def body(context, out_grad, error_in, right_init):
    rank, rows = right_init.shape[1], out_grad.shape[2]
    replicas = lax.axis_size(DP)
    core = lax.axis_index("tensor_1").astype(jnp.int32).reshape(1)
    z = exchanged(sketch(right_init, context), TENSOR)
    grads = []
    turns = turn(out_grad)
    for turned in turns:
        grads.append(lax.all_gather(turned, TENSOR, axis=0, tiled=False))
    error_part = error_sketch(right_init, error_in)
    send, keep = left_term(core, z, out_grad, error_part)
    arrived = swapped(send)
    terms = exchanged(cut(keep, arrived, lax.axis_size(WIDE)), WIDE)
    own = exchanged(sum_copies(terms, BF16), WIDE)
    other = swapped(own)
    left, w = own_tokens(core, own, other, out_grad, rank, lax.axis_size(TENSOR))
    w = exchanged(w, TENSOR)
    right = right_term(w, context, left_error(left, error_in), replicas)
    right = exchanged(right, DP)
    right = exchanged(sum_copies(right, F32), DP)
    inverse, turned = inverse_of_gram(left)
    moments = []
    for layer, grad_t in enumerate(grads):
        moments.append(moment_of(grad_t, context, error_in, layer))
    share = rows // replicas
    own_left = lax.dynamic_slice_in_dim(left, lax.axis_index(DP) * share, share, 2)
    return outputs(right, inverse, turned, own_left, moments, replicas)


def solution(mesh):
    finer = Mesh(mesh.devices.reshape(4, 8, 4, 2), ("dp_0", "dp_1", "tensor_0", "tensor_1"))
    return jax.shard_map(
        body,
        mesh=finer,
        in_specs=(
            P(None, DP, TENSOR),
            P(None, DP_TENSOR, None),
            P(None, DP, TENSOR),
            P(None, None, TENSOR),
        ),
        out_specs=(P(None, DP, TENSOR), P(None, DP, TENSOR)),
        check_vma=False,
    )
```

```python
import functools

import jax
import jax.numpy as jnp
from jax import lax
from jax.experimental import pallas as pl
from jax.experimental.pallas import tpu as pltpu
from jax.sharding import Mesh
from jax.sharding import PartitionSpec as P


TENSOR = ("tensor_0", "tensor_1")
DP_TENSOR = ("dp_0", "dp_1", "tensor_0", "tensor_1")
DP = ("dp_0", "dp_1")
WIDE = ("dp_0", "dp_1", "tensor_0")
F32, BF16 = jnp.float32, jnp.bfloat16
HIGHEST = lax.Precision.HIGHEST
VMEM = pl.BlockSpec(memory_space=pltpu.VMEM)
SMEM = pl.BlockSpec(memory_space=pltpu.SMEM)


def room(mib):
    return pltpu.CompilerParams(vmem_limit_bytes=mib * 1024 * 1024)


def cost(flops, nbytes):
    return pl.CostEstimate(flops=int(flops), bytes_accessed=int(nbytes), transcendentals=0)


def two_parts(x):
    high = x.astype(BF16)
    return high, (x - high.astype(F32)).astype(BF16)


def dot(a, b, dims, **kw):
    return lax.dot_general(a, b, (dims, ((), ())), preferred_element_type=F32, **kw)


def sketch_kernel(r_ref, x_ref, o_ref):
    rank = r_ref.shape[1]
    for layer in range(r_ref.shape[0]):
        stacked = jnp.concatenate(two_parts(r_ref[layer]), axis=0)
        z = dot(stacked, x_ref[layer], ((1,), (1,)))
        z = (z[:rank] + z[rank:]).astype(BF16)
        for j in range(o_ref.shape[0]):
            o_ref[j, layer] = z[:, j * 128 : (j + 1) * 128]


def sketch(right_init, context):
    layers, rank, _ = right_init.shape
    tokens = context.shape[1]
    return pl.pallas_call(
        sketch_kernel,
        out_shape=jax.ShapeDtypeStruct((tokens // 128, layers, rank, 128), BF16),
        in_specs=[VMEM, VMEM],
        out_specs=VMEM,
        cost_estimate=cost(4e8, 2e6),
        name="sketch",
        compiler_params=room(56),
    )(right_init, context)


def error_sketch_kernel(r_ref, e_ref, o_ref):
    rank = r_ref.shape[1]
    stacked = jnp.concatenate(two_parts(r_ref[0]), axis=0)
    z = dot(stacked, e_ref[0], ((1,), (1,)))
    o_ref[0] = z[:rank] + z[rank:]


def error_sketch(right_init, error_in):
    layers, rank, width = right_init.shape
    rows = error_in.shape[1]
    step = 768
    return pl.pallas_call(
        error_sketch_kernel,
        out_shape=jax.ShapeDtypeStruct((layers, rank, rows), F32),
        grid=(layers, rows // step),
        in_specs=[
            pl.BlockSpec((1, rank, width), lambda l, d: (l, 0, 0)),
            pl.BlockSpec((1, step, width), lambda l, d: (l, d, 0)),
        ],
        out_specs=pl.BlockSpec((1, rank, step), lambda l, d: (l, 0, d)),
        cost_estimate=cost(6e8, 7e6),
        name="error_sketch",
        compiler_params=room(6),
    )(right_init, error_in)


def left_term_kernel(core_ref, z_ref, y_ref, e_ref, send_ref, keep_ref):
    rank = z_ref.shape[2]
    core = core_ref[0]
    for which, out in ((1 - core, send_ref), (core, keep_ref)):
        z = z_ref[0, which].astype(F32)
        for j in range(1, z_ref.shape[0]):
            z = z + z_ref[j, which].astype(F32)
        t = dot(jnp.concatenate(two_parts(z), axis=0), y_ref[which], ((1,), (0,)))
        out[...] = t[:rank] + t[rank:] + e_ref[which]


def left_term(core, z, own_grad, error_part):
    rank, rows = error_part.shape[1:]
    shape = jax.ShapeDtypeStruct((rank, rows), F32)
    return pl.pallas_call(
        left_term_kernel,
        out_shape=(shape, shape),
        in_specs=[SMEM, VMEM, VMEM, VMEM],
        out_specs=(VMEM, VMEM),
        cost_estimate=cost(2e8, 5e6),
        name="left_term",
        compiler_params=room(12),
    )(core, z, own_grad, error_part)


def cut_kernel(a_ref, b_ref, o_ref):
    high, wide = o_ref.shape[1:]
    across = a_ref.shape[1] // wide
    both = (a_ref[...] + b_ref[...]).astype(BF16)
    for p in range(o_ref.shape[0]):
        i, j = divmod(p, across)
        o_ref[p] = both[i * high : i * high + high, j * wide : j * wide + wide]


def cut(a, b, pieces):
    rank, rows = a.shape
    high, wide = 4, 384
    assert pieces * high * wide == rank * rows
    return pl.pallas_call(
        cut_kernel,
        out_shape=jax.ShapeDtypeStruct((pieces, high, wide), BF16),
        in_specs=[VMEM, VMEM],
        out_specs=VMEM,
        cost_estimate=cost(4e5, 1.2e6),
        name="cut",
        compiler_params=room(6),
    )(a, b)


def sum_copies_kernel(x_ref, o_ref):
    parts = [x_ref[p].astype(F32) for p in range(4)]
    for p in range(4, x_ref.shape[0], 4):
        for q in range(4):
            parts[q] = parts[q] + x_ref[p + q].astype(F32)
    total = ((parts[0] + parts[1]) + (parts[2] + parts[3])).astype(o_ref.dtype)
    for p in range(o_ref.shape[0]):
        o_ref[p] = total


def sum_copies(x, dtype):
    return pl.pallas_call(
        sum_copies_kernel,
        out_shape=jax.ShapeDtypeStruct(x.shape, dtype),
        in_specs=[VMEM],
        out_specs=VMEM,
        cost_estimate=cost(x.size, x.size * 4),
        name="sum_copies",
        compiler_params=room(4),
    )(x)


def own_tokens_kernel(core_ref, a_ref, b_ref, y_ref, l_ref, o_ref):
    core = core_ref[0]
    high, wide = a_ref.shape[1:]
    across = l_ref.shape[2] // wide
    for which, ref in ((core, a_ref), (1 - core, b_ref)):
        rows = [
            jnp.concatenate([ref[i * across + j] for j in range(across)], axis=1)
            for i in range(l_ref.shape[1] // high)
        ]
        left = jnp.concatenate(rows, axis=0)
        l_ref[which] = left
        w = dot(left, y_ref[which], ((1,), (1,))).astype(BF16)
        for k in range(o_ref.shape[0]):
            o_ref[k, which] = w


def own_tokens(core, own, other, own_grad, rank, count):
    rows = own_grad.shape[2]
    return pl.pallas_call(
        own_tokens_kernel,
        out_shape=(
            jax.ShapeDtypeStruct((2, rank, rows), BF16),
            jax.ShapeDtypeStruct((count, 2, rank, 128), BF16),
        ),
        in_specs=[SMEM, VMEM, VMEM, VMEM],
        out_specs=(VMEM, VMEM),
        cost_estimate=cost(2e8, 4e6),
        name="own_tokens",
        compiler_params=room(6),
    )(core, own, other, own_grad)


def left_error_kernel(l_ref, e_ref, o_ref):
    for layer in range(l_ref.shape[0]):
        o_ref[layer] = dot(l_ref[layer], e_ref[layer], ((1,), (0,)))


def left_error(left, error_in):
    layers, rank, _ = left.shape
    return pl.pallas_call(
        left_error_kernel,
        out_shape=jax.ShapeDtypeStruct((layers, rank, error_in.shape[2]), F32),
        in_specs=[VMEM, VMEM],
        out_specs=VMEM,
        cost_estimate=cost(6e8, 6e6),
        name="left_error",
        compiler_params=room(10),
    )(left, error_in)


def right_term_kernel(w_ref, x_ref, e_ref, o_ref):
    layers, rank, width = e_ref.shape
    count, lanes = rank // 16, width // 128
    for layer in range(layers):
        w = jnp.concatenate([w_ref[k, layer] for k in range(w_ref.shape[0])], axis=1)
        right = dot(w, x_ref[layer], ((1,), (0,))) + e_ref[layer]
        for i in range(count):
            for j in range(lanes):
                o_ref[(layer * count + i) * lanes + j] = right[i * 16 : i * 16 + 16, j * 128 : j * 128 + 128]
    for p in range(layers * count * lanes, o_ref.shape[0]):
        o_ref[p] = jnp.zeros(o_ref.shape[1:], o_ref.dtype)


def right_term(w, context, error_part, pieces):
    return pl.pallas_call(
        right_term_kernel,
        out_shape=jax.ShapeDtypeStruct((pieces, 16, 128), F32),
        in_specs=[VMEM, VMEM, VMEM],
        out_specs=VMEM,
        cost_estimate=cost(2e8, 3e6),
        name="right_term",
        compiler_params=room(6),
    )(w, context, error_part)


def turn_kernel(y_ref, *o_refs):
    for layer, o_ref in enumerate(o_refs):
        o_ref[...] = y_ref[layer].T


def turn(own_grad):
    layers, tokens, rows = own_grad.shape
    return pl.pallas_call(
        turn_kernel,
        out_shape=[jax.ShapeDtypeStruct((rows, tokens), BF16)] * layers,
        in_specs=[VMEM],
        out_specs=[VMEM] * layers,
        cost_estimate=cost(1e8, 3e6),
        name="turn",
        compiler_params=room(58),
    )(own_grad)


def moment_kernel(core_ref, a_ref, b_ref, x_ref, e_ref, o_ref, rhs_ref):
    core = core_ref[0]
    count = a_ref.shape[0]

    @pl.when(pl.program_id(0) == 0)
    def _():
        for first, which in ((0, core), (count, 1 - core)):
            for y in range(count):
                rows = pl.ds(pl.multiple_of((2 * y + which) * 128, 128), 128)
                rhs_ref[(first + y) * 128 : (first + y) * 128 + 128] = x_ref[0, rows, :]

    grad = jnp.concatenate([ref[k] for ref in (a_ref, b_ref) for k in range(count)], axis=1)
    o_ref[...] = (dot(grad, rhs_ref[...], ((1,), (0,))) + e_ref[0].astype(F32)).astype(BF16)


def moment_of(core, own, other, context, error_in, layer):
    blocks, rows, _ = own.shape
    tokens, width = context.shape[1:]
    step = 512
    part = pl.BlockSpec((blocks, step, 128), lambda d: (0, d, 0))
    return pl.pallas_call(
        moment_kernel,
        out_shape=jax.ShapeDtypeStruct((rows, width), BF16),
        grid=(rows // step,),
        in_specs=[
            SMEM,
            part,
            part,
            pl.BlockSpec((1, tokens, width), lambda d: (layer, 0, 0)),
            pl.BlockSpec((1, step, width), lambda d: (layer, d, 0)),
        ],
        out_specs=pl.BlockSpec((step, width), lambda d: (d, 0)),
        scratch_shapes=[pltpu.VMEM((tokens, width), BF16)],
        cost_estimate=cost(4e9, 14e6),
        compiler_params=room(58),
    )(core, own, other, context, error_in)


def inverse_kernel(l_ref, o_ref, t_ref):
    rank = l_ref.shape[1]
    row = lax.broadcasted_iota(jnp.int32, (rank, 2 * rank), 0)
    col = lax.broadcasted_iota(jnp.int32, (rank, 2 * rank), 1)
    work = []
    for layer in range(l_ref.shape[0]):
        left = l_ref[layer]
        turned = left.T
        t_ref[layer] = jnp.concatenate([turned, turned], axis=1)
        gram = dot(left, left, ((1,), (1,)))
        wide = jnp.concatenate([gram, jnp.zeros((rank, rank), F32)], axis=1)
        diag = jnp.sum(jnp.where(row == col, wide, 0.0), axis=1, keepdims=True)
        ridge = 1e-6 * (jnp.sum(diag, axis=0, keepdims=True) / rank)
        wide = wide + jnp.where(row == col, ridge, 0.0)
        work.append(jnp.where(col == row + rank, 1.0, wide))
    for k in range(rank):
        for layer in range(len(work)):
            a = work[layer]
            pivot_row = a[k : k + 1, :] / a[k : k + 1, k : k + 1]
            column = a[:, k : k + 1]
            work[layer] = jnp.where(row == k, pivot_row, a - column * pivot_row)
    for layer in range(len(work)):
        o_ref[layer] = work[layer][:, rank:]


def inverse_of_gram(left):
    layers, rank, rows = left.shape
    return pl.pallas_call(
        inverse_kernel,
        out_shape=(
            jax.ShapeDtypeStruct((layers, rank, rank), F32),
            jax.ShapeDtypeStruct((layers, rows, 2 * rank), BF16),
        ),
        in_specs=[VMEM],
        out_specs=(VMEM, VMEM),
        cost_estimate=cost(5e9, 2e6),
        name="gram_inverse",
        compiler_params=room(6),
    )(left)


def outputs_kernel(r_ref, g_ref, t_ref, own_ref, m0_ref, m1_ref, s_ref, e_ref, q_ref, *, replicas):
    layer, d = pl.program_id(0), pl.program_id(1)
    rank, width = g_ref.shape[1], m0_ref.shape[1]
    count, lanes = rank // 16, width // 128

    @pl.when(d == 0)
    def _():
        rows = [
            jnp.concatenate([r_ref[(layer * count + i) * lanes + j] for j in range(lanes)], axis=1)
            for i in range(count)
        ]
        q = dot(g_ref[0], jnp.concatenate(rows, axis=0), ((1,), (0,)), precision=HIGHEST)
        own = own_ref[0]
        s = dot(jnp.concatenate([own, own], axis=0), jnp.concatenate(two_parts(q), axis=0), ((0,), (0,)))
        s_ref[0] = s.astype(BF16)
        q_ref[...] = jnp.concatenate(two_parts(q * (-1.0 / replicas)), axis=0)

    update = dot(t_ref[0], q_ref[...], ((1,), (0,)))
    for which, m_ref in ((0, m0_ref), (1, m1_ref)):

        @pl.when(layer == which)
        def _():
            e_ref[0] = (m_ref[...].astype(F32) + update).astype(BF16)


def outputs(right, inverse, turned, own_left, moments, replicas):
    rows, width = moments[0].shape
    layers, rank, share = own_left.shape
    step = 768
    last = rows // step - 1
    return pl.pallas_call(
        functools.partial(outputs_kernel, replicas=replicas),
        out_shape=(
            jax.ShapeDtypeStruct((layers, share, width), BF16),
            jax.ShapeDtypeStruct((layers, rows, width), BF16),
        ),
        grid=(layers, rows // step),
        in_specs=[
            pl.BlockSpec(right.shape, lambda l, d: (0, 0, 0)),
            pl.BlockSpec((1, rank, rank), lambda l, d: (l, 0, 0)),
            pl.BlockSpec((1, step, 2 * rank), lambda l, d: (l, d, 0)),
            pl.BlockSpec((1, rank, share), lambda l, d: (l, 0, 0)),
            pl.BlockSpec((step, width), lambda l, d: (d * (1 - l) + last * l, 0)),
            pl.BlockSpec((step, width), lambda l, d: (d * l, 0)),
        ],
        out_specs=(
            pl.BlockSpec((1, share, width), lambda l, d: (l, 0, 0)),
            pl.BlockSpec((1, step, width), lambda l, d: (l, d, 0)),
        ),
        scratch_shapes=[pltpu.VMEM((2 * rank, width), BF16)],
        cost_estimate=cost(6e8, 15e6),
        name="outputs",
        compiler_params=room(50),
    )(right, inverse, turned, own_left, *moments)


def exchanged(x, axis):
    return lax.all_to_all(x, axis, 0, 0, tiled=True)


SWAP = [(0, 1), (1, 0)]


def swapped(x):
    return lax.ppermute(x, "tensor_1", SWAP)


def body(context, out_grad, error_in, right_init):
    rank, rows = right_init.shape[1], out_grad.shape[2]
    replicas = lax.axis_size(DP)
    core = lax.axis_index("tensor_1").astype(jnp.int32).reshape(1)
    z = exchanged(sketch(right_init, context), TENSOR)
    grads = []
    turns = turn(out_grad)
    for turned in turns:
        grads.append(lax.all_gather(turned, "tensor_0", axis=0, tiled=False))
    error_part = error_sketch(right_init, error_in)
    send, keep = left_term(core, z, out_grad, error_part)
    arrived = swapped(send)
    terms = exchanged(cut(keep, arrived, lax.axis_size(WIDE)), WIDE)
    own = exchanged(sum_copies(terms, BF16), WIDE)
    other = swapped(own)
    left, w = own_tokens(core, own, other, out_grad, rank, lax.axis_size(TENSOR))
    w = exchanged(w, TENSOR)
    right = right_term(w, context, left_error(left, error_in), replicas)
    right = exchanged(right, DP)
    right = exchanged(sum_copies(right, F32), DP)
    inverse, turned = inverse_of_gram(left)
    moments = []
    for layer, grad_t in enumerate(grads):
        grad_other = swapped(grad_t)
        moments.append(moment_of(core, grad_t, grad_other, context, error_in, layer))
    share = rows // replicas
    own_left = lax.dynamic_slice_in_dim(left, lax.axis_index(DP) * share, share, 2)
    return outputs(right, inverse, turned, own_left, moments, replicas)


def solution(mesh):
    finer = Mesh(mesh.devices.reshape(4, 8, 4, 2), ("dp_0", "dp_1", "tensor_0", "tensor_1"))
    return jax.shard_map(
        body,
        mesh=finer,
        in_specs=(
            P(None, DP, TENSOR),
            P(None, DP_TENSOR, None),
            P(None, DP, TENSOR),
            P(None, None, TENSOR),
        ),
        out_specs=(P(None, DP, TENSOR), P(None, DP, TENSOR)),
        check_vma=False,
    )
```

```python
import functools

import jax
import jax.numpy as jnp
from jax import lax
from jax.experimental import pallas as pl
from jax.experimental.pallas import tpu as pltpu
from jax.sharding import Mesh
from jax.sharding import PartitionSpec as P


TENSOR = ("tensor_0", "tensor_1")
DP_TENSOR = ("dp_0", "dp_1", "tensor_0", "tensor_1")
DP = ("dp_0", "dp_1")
F32, BF16 = jnp.float32, jnp.bfloat16
HIGHEST = lax.Precision.HIGHEST
VMEM = pl.BlockSpec(memory_space=pltpu.VMEM)
SMEM = pl.BlockSpec(memory_space=pltpu.SMEM)


def room(mib):
    return pltpu.CompilerParams(vmem_limit_bytes=mib * 1024 * 1024)


def cost(flops, nbytes):
    return pl.CostEstimate(flops=int(flops), bytes_accessed=int(nbytes), transcendentals=0)


def two_parts(x):
    high = x.astype(BF16)
    return high, (x - high.astype(F32)).astype(BF16)


def dot(a, b, dims, **kw):
    return lax.dot_general(a, b, (dims, ((), ())), preferred_element_type=F32, **kw)


def sketch_kernel(r_ref, x_ref, o_ref):
    rank = r_ref.shape[1]
    for layer in range(r_ref.shape[0]):
        stacked = jnp.concatenate(two_parts(r_ref[layer]), axis=0)
        z = dot(stacked, x_ref[layer], ((1,), (1,)))
        z = (z[:rank] + z[rank:]).astype(BF16)
        for j in range(o_ref.shape[0]):
            o_ref[j, layer] = z[:, j * 128 : (j + 1) * 128]


def sketch(right_init, context):
    layers, rank, _ = right_init.shape
    tokens = context.shape[1]
    return pl.pallas_call(
        sketch_kernel,
        out_shape=jax.ShapeDtypeStruct((tokens // 128, layers, rank, 128), BF16),
        in_specs=[VMEM, VMEM],
        out_specs=VMEM,
        cost_estimate=cost(4e8, 2e6),
        name="sketch",
        compiler_params=room(56),
    )(right_init, context)


def error_sketch_kernel(r_ref, e_ref, o_ref):
    rank = r_ref.shape[1]
    stacked = jnp.concatenate(two_parts(r_ref[0]), axis=0)
    z = dot(stacked, e_ref[0], ((1,), (1,)))
    o_ref[0] = z[:rank] + z[rank:]


def error_sketch(right_init, error_in):
    layers, rank, width = right_init.shape
    rows = error_in.shape[1]
    step = 768
    return pl.pallas_call(
        error_sketch_kernel,
        out_shape=jax.ShapeDtypeStruct((layers, rank, rows), F32),
        grid=(layers, rows // step),
        in_specs=[
            pl.BlockSpec((1, rank, width), lambda l, d: (l, 0, 0)),
            pl.BlockSpec((1, step, width), lambda l, d: (l, d, 0)),
        ],
        out_specs=pl.BlockSpec((1, rank, step), lambda l, d: (l, 0, d)),
        cost_estimate=cost(6e8, 7e6),
        name="error_sketch",
        compiler_params=room(6),
    )(right_init, error_in)


def left_term_kernel(core_ref, z_ref, y_ref, e_ref, send_ref, keep_ref):
    rank = z_ref.shape[2]
    core = core_ref[0]
    for which, out in ((1 - core, send_ref), (core, keep_ref)):
        z = z_ref[0, which].astype(F32)
        for j in range(1, z_ref.shape[0]):
            z = z + z_ref[j, which].astype(F32)
        t = dot(jnp.concatenate(two_parts(z), axis=0), y_ref[which], ((1,), (0,)))
        out[...] = t[:rank] + t[rank:] + e_ref[which]


def left_term(core, z, own_grad, error_part):
    rank, rows = error_part.shape[1:]
    shape = jax.ShapeDtypeStruct((rank, rows), F32)
    return pl.pallas_call(
        left_term_kernel,
        out_shape=(shape, shape),
        in_specs=[SMEM, VMEM, VMEM, VMEM],
        out_specs=(VMEM, VMEM),
        cost_estimate=cost(2e8, 5e6),
        name="left_term",
        compiler_params=room(12),
    )(core, z, own_grad, error_part)


def cut_kernel(a_ref, b_ref, o_ref):
    high, wide = o_ref.shape[1:]
    across = a_ref.shape[1] // wide
    both = (a_ref[...] + b_ref[...]).astype(BF16)
    for p in range(o_ref.shape[0]):
        i, j = divmod(p, across)
        o_ref[p] = both[i * high : i * high + high, j * wide : j * wide + wide]


def cut(a, b, pieces):
    rank, rows = a.shape
    high, wide = 16, 384
    assert pieces * high * wide == rank * rows
    return pl.pallas_call(
        cut_kernel,
        out_shape=jax.ShapeDtypeStruct((pieces, high, wide), BF16),
        in_specs=[VMEM, VMEM],
        out_specs=VMEM,
        cost_estimate=cost(4e5, 1.2e6),
        name="cut",
        compiler_params=room(6),
    )(a, b)


def sum_copies_kernel(x_ref, o_ref):
    parts = [x_ref[p].astype(F32) for p in range(4)]
    for p in range(4, x_ref.shape[0], 4):
        for q in range(4):
            parts[q] = parts[q] + x_ref[p + q].astype(F32)
    total = ((parts[0] + parts[1]) + (parts[2] + parts[3])).astype(o_ref.dtype)
    for p in range(o_ref.shape[0]):
        o_ref[p] = total


def sum_copies(x, count, dtype):
    return pl.pallas_call(
        sum_copies_kernel,
        out_shape=jax.ShapeDtypeStruct((count, *x.shape[1:]), dtype),
        in_specs=[VMEM],
        out_specs=VMEM,
        cost_estimate=cost(x.size, x.size * 4),
        name="sum_copies",
        compiler_params=room(4),
    )(x)


def own_tokens_kernel(core_ref, a_ref, b_ref, y_ref, l_ref, o_ref):
    core = core_ref[0]
    high, wide = a_ref.shape[1:]
    across = l_ref.shape[2] // wide
    for which, ref in ((core, a_ref), (1 - core, b_ref)):
        rows = [
            jnp.concatenate([ref[i * across + j] for j in range(across)], axis=1)
            for i in range(l_ref.shape[1] // high)
        ]
        left = jnp.concatenate(rows, axis=0)
        l_ref[which] = left
        w = dot(left, y_ref[which], ((1,), (1,))).astype(BF16)
        for k in range(o_ref.shape[0]):
            o_ref[k, which] = w


def own_tokens(core, own, other, own_grad, rank, count):
    rows = own_grad.shape[2]
    return pl.pallas_call(
        own_tokens_kernel,
        out_shape=(
            jax.ShapeDtypeStruct((2, rank, rows), BF16),
            jax.ShapeDtypeStruct((count, 2, rank, 128), BF16),
        ),
        in_specs=[SMEM, VMEM, VMEM, VMEM],
        out_specs=(VMEM, VMEM),
        cost_estimate=cost(2e8, 4e6),
        name="own_tokens",
        compiler_params=room(6),
    )(core, own, other, own_grad)


def left_error_kernel(l_ref, e_ref, o_ref):
    for layer in range(l_ref.shape[0]):
        o_ref[layer] = dot(l_ref[layer], e_ref[layer], ((1,), (0,)))


def left_error(left, error_in):
    layers, rank, _ = left.shape
    return pl.pallas_call(
        left_error_kernel,
        out_shape=jax.ShapeDtypeStruct((layers, rank, error_in.shape[2]), F32),
        in_specs=[VMEM, VMEM],
        out_specs=VMEM,
        cost_estimate=cost(6e8, 6e6),
        name="left_error",
        compiler_params=room(10),
    )(left, error_in)


def right_term_kernel(w_ref, x_ref, e_ref, o_ref):
    layers, rank, width = e_ref.shape
    count, lanes = rank // 16, width // 128
    for layer in range(layers):
        w = jnp.concatenate([w_ref[k, layer] for k in range(w_ref.shape[0])], axis=1)
        right = dot(w, x_ref[layer], ((1,), (0,))) + e_ref[layer]
        for i in range(count):
            for j in range(lanes):
                o_ref[(layer * count + i) * lanes + j] = right[i * 16 : i * 16 + 16, j * 128 : j * 128 + 128]
    for p in range(layers * count * lanes, o_ref.shape[0]):
        o_ref[p] = jnp.zeros(o_ref.shape[1:], o_ref.dtype)


def right_term(w, context, error_part, pieces):
    return pl.pallas_call(
        right_term_kernel,
        out_shape=jax.ShapeDtypeStruct((pieces, 16, 128), F32),
        in_specs=[VMEM, VMEM, VMEM],
        out_specs=VMEM,
        cost_estimate=cost(2e8, 3e6),
        name="right_term",
        compiler_params=room(6),
    )(w, context, error_part)


def turn_kernel(y_ref, *o_refs):
    for layer, o_ref in enumerate(o_refs):
        o_ref[...] = y_ref[layer].T


def turn(own_grad):
    layers, tokens, rows = own_grad.shape
    return pl.pallas_call(
        turn_kernel,
        out_shape=[jax.ShapeDtypeStruct((rows, tokens), BF16)] * layers,
        in_specs=[VMEM],
        out_specs=[VMEM] * layers,
        cost_estimate=cost(1e8, 3e6),
        name="turn",
        compiler_params=room(8),
    )(own_grad)


def moment_kernel(y_ref, x_ref, e_ref, o_ref):
    y = jnp.concatenate([y_ref[k] for k in range(y_ref.shape[0])], axis=1)
    o_ref[...] = (dot(y, x_ref[0], ((1,), (0,))) + e_ref[0].astype(F32)).astype(BF16)


def moment_of(grad_t, context, error_in, layer):
    blocks, rows, _ = grad_t.shape
    tokens, width = context.shape[1:]
    step = 512
    return pl.pallas_call(
        moment_kernel,
        out_shape=jax.ShapeDtypeStruct((rows, width), BF16),
        grid=(rows // step,),
        in_specs=[
            pl.BlockSpec((blocks, step, 128), lambda d: (0, d, 0)),
            pl.BlockSpec((1, tokens, width), lambda d: (layer, 0, 0)),
            pl.BlockSpec((1, step, width), lambda d: (layer, d, 0)),
        ],
        out_specs=pl.BlockSpec((step, width), lambda d: (d, 0)),
        cost_estimate=cost(4e9, 14e6),
        compiler_params=room(56),
    )(grad_t, context, error_in)


def inverse_kernel(l_ref, o_ref, t_ref):
    rank = l_ref.shape[1]
    row = lax.broadcasted_iota(jnp.int32, (rank, 2 * rank), 0)
    col = lax.broadcasted_iota(jnp.int32, (rank, 2 * rank), 1)
    work = []
    for layer in range(l_ref.shape[0]):
        left = l_ref[layer]
        turned = left.T
        t_ref[layer] = jnp.concatenate([turned, turned], axis=1)
        gram = dot(left, left, ((1,), (1,)))
        wide = jnp.concatenate([gram, jnp.zeros((rank, rank), F32)], axis=1)
        diag = jnp.sum(jnp.where(row == col, wide, 0.0), axis=1, keepdims=True)
        ridge = 1e-6 * (jnp.sum(diag, axis=0, keepdims=True) / rank)
        wide = wide + jnp.where(row == col, ridge, 0.0)
        work.append(jnp.where(col == row + rank, 1.0, wide))
    for k in range(rank):
        for layer in range(len(work)):
            a = work[layer]
            pivot_row = a[k : k + 1, :] / a[k : k + 1, k : k + 1]
            column = a[:, k : k + 1]
            work[layer] = jnp.where(row == k, pivot_row, a - column * pivot_row)
    for layer in range(len(work)):
        o_ref[layer] = work[layer][:, rank:]


def inverse_of_gram(left):
    layers, rank, rows = left.shape
    return pl.pallas_call(
        inverse_kernel,
        out_shape=(
            jax.ShapeDtypeStruct((layers, rank, rank), F32),
            jax.ShapeDtypeStruct((layers, rows, 2 * rank), BF16),
        ),
        in_specs=[VMEM],
        out_specs=(VMEM, VMEM),
        cost_estimate=cost(5e9, 2e6),
        name="gram_inverse",
        compiler_params=room(6),
    )(left)


def outputs_kernel(r_ref, g_ref, t_ref, own_ref, m0_ref, m1_ref, s_ref, e_ref, q_ref, *, replicas):
    layer, d = pl.program_id(0), pl.program_id(1)
    rank, width = g_ref.shape[1], m0_ref.shape[1]
    count, lanes = rank // 16, width // 128

    @pl.when(d == 0)
    def _():
        rows = [
            jnp.concatenate([r_ref[(layer * count + i) * lanes + j] for j in range(lanes)], axis=1)
            for i in range(count)
        ]
        q = dot(g_ref[0], jnp.concatenate(rows, axis=0), ((1,), (0,)), precision=HIGHEST)
        own = own_ref[0]
        s = dot(jnp.concatenate([own, own], axis=0), jnp.concatenate(two_parts(q), axis=0), ((0,), (0,)))
        s_ref[0] = s.astype(BF16)
        q_ref[...] = jnp.concatenate(two_parts(q * (-1.0 / replicas)), axis=0)

    update = dot(t_ref[0], q_ref[...], ((1,), (0,)))
    for which, m_ref in ((0, m0_ref), (1, m1_ref)):

        @pl.when(layer == which)
        def _():
            e_ref[0] = (m_ref[...].astype(F32) + update).astype(BF16)


def outputs(right, inverse, turned, own_left, moments, replicas):
    rows, width = moments[0].shape
    layers, rank, share = own_left.shape
    step = 768
    last = rows // step - 1
    return pl.pallas_call(
        functools.partial(outputs_kernel, replicas=replicas),
        out_shape=(
            jax.ShapeDtypeStruct((layers, share, width), BF16),
            jax.ShapeDtypeStruct((layers, rows, width), BF16),
        ),
        grid=(layers, rows // step),
        in_specs=[
            pl.BlockSpec(right.shape, lambda l, d: (0, 0, 0)),
            pl.BlockSpec((1, rank, rank), lambda l, d: (l, 0, 0)),
            pl.BlockSpec((1, step, 2 * rank), lambda l, d: (l, d, 0)),
            pl.BlockSpec((1, rank, share), lambda l, d: (l, 0, 0)),
            pl.BlockSpec((step, width), lambda l, d: (d * (1 - l) + last * l, 0)),
            pl.BlockSpec((step, width), lambda l, d: (d * l, 0)),
        ],
        out_specs=(
            pl.BlockSpec((1, share, width), lambda l, d: (l, 0, 0)),
            pl.BlockSpec((1, step, width), lambda l, d: (l, d, 0)),
        ),
        scratch_shapes=[pltpu.VMEM((2 * rank, width), BF16)],
        cost_estimate=cost(6e8, 15e6),
        name="outputs",
        compiler_params=room(50),
    )(right, inverse, turned, own_left, *moments)


def exchanged(x, axis):
    return lax.all_to_all(x, axis, 0, 0, tiled=True)


SWAP = [(0, 1), (1, 0)]


def swapped(x):
    return lax.ppermute(x, "tensor_1", SWAP)


def body(context, out_grad, error_in, right_init):
    rank, rows = right_init.shape[1], out_grad.shape[2]
    replicas = lax.axis_size(DP)
    core = lax.axis_index("tensor_1").astype(jnp.int32).reshape(1)
    z = exchanged(sketch(right_init, context), TENSOR)
    grads = []
    turns = turn(out_grad)
    for turned in turns:
        grads.append(lax.all_gather(turned, TENSOR, axis=0, tiled=False))
    error_part = error_sketch(right_init, error_in)
    send, keep = left_term(core, z, out_grad, error_part)
    arrived = swapped(send)
    terms = exchanged(cut(keep, arrived, replicas), DP)
    terms = exchanged(sum_copies(terms, lax.axis_size("tensor_0"), F32), "tensor_0")
    own = exchanged(sum_copies(terms, replicas, BF16), DP)
    other = swapped(own)
    left, w = own_tokens(core, own, other, out_grad, rank, lax.axis_size(TENSOR))
    w = exchanged(w, TENSOR)
    right = right_term(w, context, left_error(left, error_in), replicas)
    right = exchanged(right, DP)
    right = exchanged(sum_copies(right, replicas, F32), DP)
    inverse, turned = inverse_of_gram(left)
    moments = []
    for layer, grad_t in enumerate(grads):
        moments.append(moment_of(grad_t, context, error_in, layer))
    share = rows // replicas
    own_left = lax.dynamic_slice_in_dim(left, lax.axis_index(DP) * share, share, 2)
    return outputs(right, inverse, turned, own_left, moments, replicas)


def solution(mesh):
    finer = Mesh(mesh.devices.reshape(4, 8, 4, 2), ("dp_0", "dp_1", "tensor_0", "tensor_1"))
    return jax.shard_map(
        body,
        mesh=finer,
        in_specs=(
            P(None, DP, TENSOR),
            P(None, DP_TENSOR, None),
            P(None, DP, TENSOR),
            P(None, None, TENSOR),
        ),
        out_specs=(P(None, DP, TENSOR), P(None, DP, TENSOR)),
        check_vma=False,
    )
```

```python
import functools

import jax
import jax.numpy as jnp
from jax import lax
from jax.experimental import pallas as pl
from jax.experimental.pallas import tpu as pltpu
from jax.sharding import Mesh
from jax.sharding import PartitionSpec as P


TENSOR = ("tensor_0", "tensor_1")
DP_TENSOR = ("dp_0", "dp_1", "tensor_0", "tensor_1")
DP = ("dp_0", "dp_1")
F32, BF16 = jnp.float32, jnp.bfloat16
HIGHEST = lax.Precision.HIGHEST
VMEM = pl.BlockSpec(memory_space=pltpu.VMEM)
SMEM = pl.BlockSpec(memory_space=pltpu.SMEM)


def room(mib):
    return pltpu.CompilerParams(vmem_limit_bytes=mib * 1024 * 1024)


def cost(flops, nbytes):
    return pl.CostEstimate(flops=int(flops), bytes_accessed=int(nbytes), transcendentals=0)


def two_parts(x):
    high = x.astype(BF16)
    return high, (x - high.astype(F32)).astype(BF16)


def dot(a, b, dims, **kw):
    return lax.dot_general(a, b, (dims, ((), ())), preferred_element_type=F32, **kw)


def sketch_kernel(r_ref, x_ref, o_ref):
    rank = r_ref.shape[1]
    for layer in range(r_ref.shape[0]):
        stacked = jnp.concatenate(two_parts(r_ref[layer]), axis=0)
        z = dot(stacked, x_ref[layer], ((1,), (1,)))
        z = (z[:rank] + z[rank:]).astype(BF16)
        for j in range(o_ref.shape[0]):
            o_ref[j, layer] = z[:, j * 128 : (j + 1) * 128]


def sketch(right_init, context):
    layers, rank, _ = right_init.shape
    tokens = context.shape[1]
    return pl.pallas_call(
        sketch_kernel,
        out_shape=jax.ShapeDtypeStruct((tokens // 128, layers, rank, 128), BF16),
        in_specs=[VMEM, VMEM],
        out_specs=VMEM,
        cost_estimate=cost(4e8, 2e6),
        name="sketch",
        compiler_params=room(56),
    )(right_init, context)


def error_sketch_kernel(r_ref, e_ref, o_ref):
    rank = r_ref.shape[1]
    stacked = jnp.concatenate(two_parts(r_ref[0]), axis=0)
    z = dot(stacked, e_ref[0], ((1,), (1,)))
    o_ref[0] = z[:rank] + z[rank:]


def error_sketch(right_init, error_in):
    layers, rank, width = right_init.shape
    rows = error_in.shape[1]
    step = 768
    return pl.pallas_call(
        error_sketch_kernel,
        out_shape=jax.ShapeDtypeStruct((layers, rank, rows), F32),
        grid=(layers, rows // step),
        in_specs=[
            pl.BlockSpec((1, rank, width), lambda l, d: (l, 0, 0)),
            pl.BlockSpec((1, step, width), lambda l, d: (l, d, 0)),
        ],
        out_specs=pl.BlockSpec((1, rank, step), lambda l, d: (l, 0, d)),
        cost_estimate=cost(6e8, 7e6),
        name="error_sketch",
        compiler_params=room(6),
    )(right_init, error_in)


def left_term_kernel(core_ref, z_ref, y_ref, e_ref, send_ref, keep_ref):
    rank = z_ref.shape[2]
    core = core_ref[0]
    for which, out in ((1 - core, send_ref), (core, keep_ref)):
        z = z_ref[0, which].astype(F32)
        for j in range(1, z_ref.shape[0]):
            z = z + z_ref[j, which].astype(F32)
        t = dot(jnp.concatenate(two_parts(z), axis=0), y_ref[which], ((1,), (0,)))
        out[...] = t[:rank] + t[rank:] + e_ref[which]


def left_term(core, z, own_grad, error_part):
    rank, rows = error_part.shape[1:]
    shape = jax.ShapeDtypeStruct((rank, rows), F32)
    return pl.pallas_call(
        left_term_kernel,
        out_shape=(shape, shape),
        in_specs=[SMEM, VMEM, VMEM, VMEM],
        out_specs=(VMEM, VMEM),
        cost_estimate=cost(2e8, 5e6),
        name="left_term",
        compiler_params=room(12),
    )(core, z, own_grad, error_part)


def cut_kernel(a_ref, b_ref, o_ref):
    high, wide = o_ref.shape[1:]
    across = a_ref.shape[1] // wide
    both = (a_ref[...] + b_ref[...]).astype(BF16)
    for p in range(o_ref.shape[0]):
        i, j = divmod(p, across)
        o_ref[p] = both[i * high : i * high + high, j * wide : j * wide + wide]


def cut(a, b, pieces):
    rank, rows = a.shape
    high, wide = 16, 384
    assert pieces * high * wide == rank * rows
    return pl.pallas_call(
        cut_kernel,
        out_shape=jax.ShapeDtypeStruct((pieces, high, wide), BF16),
        in_specs=[VMEM, VMEM],
        out_specs=VMEM,
        cost_estimate=cost(4e5, 1.2e6),
        name="cut",
        compiler_params=room(6),
    )(a, b)


def sum_copies_kernel(x_ref, o_ref):
    parts = [x_ref[p].astype(F32) for p in range(4)]
    for p in range(4, x_ref.shape[0], 4):
        for q in range(4):
            parts[q] = parts[q] + x_ref[p + q].astype(F32)
    total = ((parts[0] + parts[1]) + (parts[2] + parts[3])).astype(o_ref.dtype)
    for p in range(o_ref.shape[0]):
        o_ref[p] = total


def sum_copies(x, count, dtype):
    return pl.pallas_call(
        sum_copies_kernel,
        out_shape=jax.ShapeDtypeStruct((count, *x.shape[1:]), dtype),
        in_specs=[VMEM],
        out_specs=VMEM,
        cost_estimate=cost(x.size, x.size * 4),
        name="sum_copies",
        compiler_params=room(4),
    )(x)


def own_tokens_kernel(core_ref, a_ref, b_ref, y_ref, l_ref, o_ref):
    core = core_ref[0]
    high, wide = a_ref.shape[1:]
    across = l_ref.shape[2] // wide
    for which, ref in ((core, a_ref), (1 - core, b_ref)):
        rows = [
            jnp.concatenate([ref[i * across + j] for j in range(across)], axis=1)
            for i in range(l_ref.shape[1] // high)
        ]
        left = jnp.concatenate(rows, axis=0)
        l_ref[which] = left
        w = dot(left, y_ref[which], ((1,), (1,))).astype(BF16)
        for k in range(o_ref.shape[0]):
            o_ref[k, which] = w


def own_tokens(core, own, other, own_grad, rank, count):
    rows = own_grad.shape[2]
    return pl.pallas_call(
        own_tokens_kernel,
        out_shape=(
            jax.ShapeDtypeStruct((2, rank, rows), BF16),
            jax.ShapeDtypeStruct((count, 2, rank, 128), BF16),
        ),
        in_specs=[SMEM, VMEM, VMEM, VMEM],
        out_specs=(VMEM, VMEM),
        cost_estimate=cost(2e8, 4e6),
        name="own_tokens",
        compiler_params=room(6),
    )(core, own, other, own_grad)


def left_error_kernel(l_ref, e_ref, o_ref):
    for layer in range(l_ref.shape[0]):
        o_ref[layer] = dot(l_ref[layer], e_ref[layer], ((1,), (0,)))


def left_error(left, error_in):
    layers, rank, _ = left.shape
    return pl.pallas_call(
        left_error_kernel,
        out_shape=jax.ShapeDtypeStruct((layers, rank, error_in.shape[2]), F32),
        in_specs=[VMEM, VMEM],
        out_specs=VMEM,
        cost_estimate=cost(6e8, 6e6),
        name="left_error",
        compiler_params=room(10),
    )(left, error_in)


def right_term_kernel(w_ref, x_ref, e_ref, o_ref):
    layers, rank, _ = e_ref.shape
    high = o_ref.shape[1]
    for layer in range(layers):
        w = jnp.concatenate([w_ref[k, layer] for k in range(w_ref.shape[0])], axis=1)
        right = (dot(w, x_ref[layer], ((1,), (0,))) + e_ref[layer]).astype(BF16)
        for i in range(rank // high):
            o_ref[layer * (rank // high) + i] = right[i * high : i * high + high]


def right_term(w, context, error_part, pieces):
    layers, rank, width = error_part.shape
    high = layers * rank // pieces
    return pl.pallas_call(
        right_term_kernel,
        out_shape=jax.ShapeDtypeStruct((pieces, high, width), BF16),
        in_specs=[VMEM, VMEM, VMEM],
        out_specs=VMEM,
        cost_estimate=cost(2e8, 3e6),
        name="right_term",
        compiler_params=room(6),
    )(w, context, error_part)


def turn_kernel(y_ref, *o_refs):
    for layer, o_ref in enumerate(o_refs):
        o_ref[...] = y_ref[layer].T


def turn(own_grad):
    layers, tokens, rows = own_grad.shape
    return pl.pallas_call(
        turn_kernel,
        out_shape=[jax.ShapeDtypeStruct((rows, tokens), BF16)] * layers,
        in_specs=[VMEM],
        out_specs=[VMEM] * layers,
        cost_estimate=cost(1e8, 3e6),
        name="turn",
        compiler_params=room(8),
    )(own_grad)


def moment_kernel(y_ref, x_ref, e_ref, o_ref):
    y = jnp.concatenate([y_ref[k] for k in range(y_ref.shape[0])], axis=1)
    o_ref[...] = (dot(y, x_ref[0], ((1,), (0,))) + e_ref[0].astype(F32)).astype(BF16)


def moment_of(grad_t, context, error_in, layer):
    blocks, rows, _ = grad_t.shape
    tokens, width = context.shape[1:]
    step = 512
    return pl.pallas_call(
        moment_kernel,
        out_shape=jax.ShapeDtypeStruct((rows, width), BF16),
        grid=(rows // step,),
        in_specs=[
            pl.BlockSpec((blocks, step, 128), lambda d: (0, d, 0)),
            pl.BlockSpec((1, tokens, width), lambda d: (layer, 0, 0)),
            pl.BlockSpec((1, step, width), lambda d: (layer, d, 0)),
        ],
        out_specs=pl.BlockSpec((step, width), lambda d: (d, 0)),
        cost_estimate=cost(4e9, 14e6),
        compiler_params=room(56),
    )(grad_t, context, error_in)


def inverse_kernel(l_ref, o_ref, t_ref):
    rank = l_ref.shape[1]
    row = lax.broadcasted_iota(jnp.int32, (rank, 2 * rank), 0)
    col = lax.broadcasted_iota(jnp.int32, (rank, 2 * rank), 1)
    work = []
    for layer in range(l_ref.shape[0]):
        left = l_ref[layer]
        turned = left.T
        t_ref[layer] = jnp.concatenate([turned, turned], axis=1)
        gram = dot(left, left, ((1,), (1,)))
        wide = jnp.concatenate([gram, jnp.zeros((rank, rank), F32)], axis=1)
        diag = jnp.sum(jnp.where(row == col, wide, 0.0), axis=1, keepdims=True)
        ridge = 1e-6 * (jnp.sum(diag, axis=0, keepdims=True) / rank)
        wide = wide + jnp.where(row == col, ridge, 0.0)
        work.append(jnp.where(col == row + rank, 1.0, wide))
    for k in range(rank):
        for layer in range(len(work)):
            a = work[layer]
            pivot_row = a[k : k + 1, :] / a[k : k + 1, k : k + 1]
            column = a[:, k : k + 1]
            work[layer] = jnp.where(row == k, pivot_row, a - column * pivot_row)
    for layer in range(len(work)):
        o_ref[layer] = work[layer][:, rank:]


def inverse_of_gram(left):
    layers, rank, rows = left.shape
    return pl.pallas_call(
        inverse_kernel,
        out_shape=(
            jax.ShapeDtypeStruct((layers, rank, rank), F32),
            jax.ShapeDtypeStruct((layers, rows, 2 * rank), BF16),
        ),
        in_specs=[VMEM],
        out_specs=(VMEM, VMEM),
        cost_estimate=cost(5e9, 2e6),
        name="gram_inverse",
        compiler_params=room(6),
    )(left)


def outputs_kernel(r_ref, g_ref, t_ref, own_ref, m0_ref, m1_ref, s_ref, e_ref, q_ref, *, replicas):
    layer, d = pl.program_id(0), pl.program_id(1)
    rank = g_ref.shape[1]
    count = rank // r_ref.shape[1]

    @pl.when(d == 0)
    def _():
        rows = [r_ref[layer * count + i] for i in range(count)]
        q = dot(g_ref[0], jnp.concatenate(rows, axis=0), ((1,), (0,)), precision=HIGHEST)
        own = own_ref[0]
        s = dot(jnp.concatenate([own, own], axis=0), jnp.concatenate(two_parts(q), axis=0), ((0,), (0,)))
        s_ref[0] = s.astype(BF16)
        q_ref[...] = jnp.concatenate(two_parts(q * (-1.0 / replicas)), axis=0)

    update = dot(t_ref[0], q_ref[...], ((1,), (0,)))
    for which, m_ref in ((0, m0_ref), (1, m1_ref)):

        @pl.when(layer == which)
        def _():
            e_ref[0] = (m_ref[...].astype(F32) + update).astype(BF16)


def outputs(right, inverse, turned, own_left, moments, replicas):
    rows, width = moments[0].shape
    layers, rank, share = own_left.shape
    step = 768
    last = rows // step - 1
    return pl.pallas_call(
        functools.partial(outputs_kernel, replicas=replicas),
        out_shape=(
            jax.ShapeDtypeStruct((layers, share, width), BF16),
            jax.ShapeDtypeStruct((layers, rows, width), BF16),
        ),
        grid=(layers, rows // step),
        in_specs=[
            pl.BlockSpec(right.shape, lambda l, d: (0, 0, 0)),
            pl.BlockSpec((1, rank, rank), lambda l, d: (l, 0, 0)),
            pl.BlockSpec((1, step, 2 * rank), lambda l, d: (l, d, 0)),
            pl.BlockSpec((1, rank, share), lambda l, d: (l, 0, 0)),
            pl.BlockSpec((step, width), lambda l, d: (d * (1 - l) + last * l, 0)),
            pl.BlockSpec((step, width), lambda l, d: (d * l, 0)),
        ],
        out_specs=(
            pl.BlockSpec((1, share, width), lambda l, d: (l, 0, 0)),
            pl.BlockSpec((1, step, width), lambda l, d: (l, d, 0)),
        ),
        scratch_shapes=[pltpu.VMEM((2 * rank, width), BF16)],
        cost_estimate=cost(6e8, 15e6),
        name="outputs",
        compiler_params=room(50),
    )(right, inverse, turned, own_left, *moments)


def exchanged(x, axis):
    return lax.all_to_all(x, axis, 0, 0, tiled=True)


SWAP = [(0, 1), (1, 0)]


def swapped(x):
    return lax.ppermute(x, "tensor_1", SWAP)


def body(context, out_grad, error_in, right_init):
    rank, rows = right_init.shape[1], out_grad.shape[2]
    replicas = lax.axis_size(DP)
    core = lax.axis_index("tensor_1").astype(jnp.int32).reshape(1)
    z = exchanged(sketch(right_init, context), TENSOR)
    grads = []
    turns = turn(out_grad)
    for turned in turns:
        grads.append(lax.all_gather(turned, TENSOR, axis=0, tiled=False))
    error_part = error_sketch(right_init, error_in)
    send, keep = left_term(core, z, out_grad, error_part)
    arrived = swapped(send)
    terms = exchanged(cut(keep, arrived, replicas), DP)
    terms = exchanged(sum_copies(terms, lax.axis_size("tensor_0"), F32), "tensor_0")
    own = exchanged(sum_copies(terms, replicas, BF16), DP)
    other = swapped(own)
    left, w = own_tokens(core, own, other, out_grad, rank, lax.axis_size(TENSOR))
    w = exchanged(w, TENSOR)
    right = right_term(w, context, left_error(left, error_in), replicas)
    right = exchanged(right, DP)
    right = exchanged(sum_copies(right, replicas, F32), DP)
    inverse, turned = inverse_of_gram(left)
    moments = []
    for layer, grad_t in enumerate(grads):
        moments.append(moment_of(grad_t, context, error_in, layer))
    share = rows // replicas
    own_left = lax.dynamic_slice_in_dim(left, lax.axis_index(DP) * share, share, 2)
    return outputs(right, inverse, turned, own_left, moments, replicas)


def solution(mesh):
    finer = Mesh(mesh.devices.reshape(4, 8, 4, 2), ("dp_0", "dp_1", "tensor_0", "tensor_1"))
    return jax.shard_map(
        body,
        mesh=finer,
        in_specs=(
            P(None, DP, TENSOR),
            P(None, DP_TENSOR, None),
            P(None, DP, TENSOR),
            P(None, None, TENSOR),
        ),
        out_specs=(P(None, DP, TENSOR), P(None, DP, TENSOR)),
        check_vma=False,
    )
```
